32 devices in a mesh: col: 4 (over z), dp: 4 (over x, core), strip: 2 (over y).
Axes of the slice: x: 2, y: 2, z: 4, core: 2. Of those that a mesh axis runs over, the one named last changes fastest.
Arguments:
- stem: bfloat16 [16, 4, 32, 360], P('dp', 'strip'), may hold values from -6 to 6
- labels: int32 [16, 4, 32], P('dp', 'strip'), may hold values from 0 to 149
- up_proj: bfloat16 [4, 720, 360], P('col'), may hold values from -0.21875 to 0.21875
- mix_proj: bfloat16 [4, 360, 360], P('col'), may hold values from -0.3125 to 0.3125
- down_proj: bfloat16 [4, 360, 720], P('col'), may hold values from -0.3125 to 0.3125
- dw_kernel: bfloat16 [4, 9, 360], P('col'), may hold values from -2 to 2
- gain1: float32 [4, 360], P('col'), may hold values from 0.31622776 to 1
- gain2: float32 [4, 720], P('col'), may hold values from 0.31622776 to 1
- lat_one: bfloat16 [360, 512], replicated, may hold values from -0.3125 to 0.3125
- lat_two: bfloat16 [720, 512], replicated, may hold values from -0.21875 to 0.21875
- classifier: bfloat16 [512, 150], replicated, may hold values from -1.0546875 to 1.0546875
Outputs:
- grad_up: float32 [4, 720, 360], P('col', ('dp', 'strip'))
- grad_mix: float32 [4, 360, 360], P('col', ('dp', 'strip'))
- grad_down: float32 [4, 360, 720], P('col', ('dp', 'strip'))
- grad_kernel: float32 [4, 9, 360], P('col', None, ('dp', 'strip'))
- grad_stem: float32 [16, 4, 32, 360], P('dp', 'strip', 'col')
The draws below stay inside these ranges and needn't reach their ends.
All inputs are finite; a program needn't handle non-finite values.
Results may differ from the reference program's by a relative error of at most 0.034.
Values sent between devices are 32-bit elements; how exact they have to be, the bound alone decides.
A program may use at most 64 MiB of HBM per device.

```python
import math
import jax
import jax.numpy as jnp
from jax import lax

C1 = 360
C2 = 720
HEAD = 512
CLASSES = 150
W1 = 32
COLS = 4
BATCH = 16
H1 = 4


def plant(values, own_key, smallest, largest):
    longest = values.shape.index(max(values.shape))
    spots = []
    for shift in (0, 1):
        where = [jax.random.randint(jax.random.fold_in(own_key, axis), (), 0, length) for axis, length in enumerate(values.shape)]
        where[longest] = (where[longest] + shift) % values.shape[longest]
        spots.append(tuple(where))
    return values.at[spots[0]].set(smallest).at[spots[1]].set(largest)


def shard_levels(own_key, shape, cuts, low, top_value):
    def one(axis_at, parts):
        steps = jax.random.uniform(jax.random.fold_in(jax.random.fold_in(own_key, 6), axis_at), (parts,), jnp.float32, low / len(cuts), top_value / len(cuts))
        return jnp.repeat(jnp.exp(steps), shape[axis_at] // parts).reshape((-1,) + (1,) * (len(shape) - axis_at - 1))

    level = one(*cuts[0])
    for cut in cuts[1:]:
        level = level * one(*cut)
    return level


def noise(own_key, dims, scale, limit, cuts=(), kind=jnp.bfloat16):
    values = jax.random.normal(own_key, dims, jnp.float32) * scale
    if len(cuts) > 0:
        values = shard_levels(own_key, dims, cuts, -0.22, 0.18) * values
    return jnp.clip(values, min=-limit, max=limit).astype(kind)


def setup_inputs(seed: int = 0) -> dict:
    arg_keys = jax.random.split(jax.random.key(seed), 12)
    return {
        "stem": noise(arg_keys[0], (BATCH, H1, W1, C1), 1.0, 6.0, ((0, 4), (1, 2))),
        "labels": plant(jax.random.randint(arg_keys[1], (BATCH, H1, W1), 0, CLASSES), jax.random.fold_in(arg_keys[1], 1), 0, CLASSES - 1).astype(jnp.int32),
        "up_proj": noise(arg_keys[2], (COLS, C2, C1), C2 ** -0.5, 0.21875, ((0, 4),)),
        "mix_proj": noise(arg_keys[3], (COLS, C1, C1), C1 ** -0.5, 0.3125, ((0, 4),)),
        "down_proj": noise(arg_keys[4], (COLS, C1, C2), C1 ** -0.5, 0.3125, ((0, 4),)),
        "dw_kernel": noise(arg_keys[5], (COLS, 9, C1), 9 ** -0.5, 2.0, ((0, 4),)),
        "gain1": jnp.clip(jnp.exp(math.log(1.0) - 1.1512926 * jax.random.uniform(arg_keys[6], (COLS, C1), jnp.float32) ** shard_levels(arg_keys[6], (COLS, C1), ((0, 4),), -0.2, 0.2)), 0.31622776, 1.0),
        "gain2": jnp.clip(jnp.exp(math.log(1.0) - 1.1512926 * jax.random.uniform(arg_keys[7], (COLS, C2), jnp.float32) ** shard_levels(arg_keys[7], (COLS, C2), ((0, 4),), -0.2, 0.2)), 0.31622776, 1.0),
        "lat_one": noise(arg_keys[8], (C1, HEAD), C1 ** -0.5, 0.3125),
        "lat_two": noise(arg_keys[9], (C2, HEAD), C2 ** -0.5, 0.21875),
        "classifier": noise(arg_keys[10], (HEAD, CLASSES), (4.0 / HEAD ** 0.5), 1.0546875),
    }


loss_scale = 64.0
root_coef = 0.7978845608028654
cube_coef = 0.044715


def gelu_pair(values):
    inner = root_coef * (values + cube_coef * values * values * values)
    tangent = jnp.tanh(inner)
    result = 0.5 * values * (1.0 + tangent)
    slope = 0.5 * (1.0 + tangent) + 0.5 * values * (1.0 - tangent * tangent) * root_coef * (1.0 + 3.0 * cube_coef * values * values)
    return result, slope


def project(left, matrix):
    flat = left.reshape(-1, left.shape[-1])
    out = jnp.dot(flat, matrix, preferred_element_type=jnp.float32)
    return out.reshape(left.shape[:-1] + (matrix.shape[1],))


def project_back(left, matrix):
    flat = left.reshape(-1, left.shape[-1])
    out = lax.dot_general(flat, matrix, (((1,), (1,)), ((), ())), preferred_element_type=jnp.float32)
    return out.reshape(left.shape[:-1] + (matrix.shape[0],))


def outer_sum(left, right):
    return lax.dot_general(left.reshape(-1, left.shape[-1]), right.reshape(-1, right.shape[-1]), (((0,), (0,)), ((), ())), preferred_element_type=jnp.float32)


def upsample(values):
    return jnp.repeat(jnp.repeat(values, 2, axis=-3), 2, axis=-2)


def pool_sum(values):
    shape = values.shape
    return values.reshape(shape[:-3] + (shape[-3] // 2, 2, shape[-2] // 2, 2, shape[-1])).sum(axis=(-4, -2))


def depthwise_apply(padded, kernel):
    row_count = padded.shape[-3] - 2
    col_count = padded.shape[-2] - 2
    total = jnp.zeros(padded.shape[:-3] + (row_count, col_count, padded.shape[-1]), jnp.float32)
    for tap_index in range(9):
        row_shift = tap_index // 3 - 1
        col_shift = tap_index % 3 - 1
        total = total + kernel[tap_index] * padded[..., 1 + row_shift:1 + row_shift + row_count, 1 + col_shift:1 + col_shift + col_count, :]
    return total


def depthwise_adjoint(padded, kernel):
    row_count = padded.shape[-3] - 2
    col_count = padded.shape[-2] - 2
    total = jnp.zeros(padded.shape[:-3] + (row_count, col_count, padded.shape[-1]), jnp.float32)
    for tap_index in range(9):
        row_shift = tap_index // 3 - 1
        col_shift = tap_index % 3 - 1
        total = total + kernel[tap_index] * padded[..., 1 - row_shift:1 - row_shift + row_count, 1 - col_shift:1 - col_shift + col_count, :]
    return total


def kernel_terms(padded, grad_depth):
    row_count = grad_depth.shape[-3]
    col_count = grad_depth.shape[-2]
    axes = tuple(range(grad_depth.ndim - 1))
    pieces = []
    for tap_index in range(9):
        row_shift = tap_index // 3 - 1
        col_shift = tap_index % 3 - 1
        window = padded[..., 1 + row_shift:1 + row_shift + row_count, 1 + col_shift:1 + col_shift + col_count, :]
        pieces.append(jnp.sum(window * grad_depth, axis=axes))
    return jnp.stack(pieces, axis=0)


def head_grads(level_one, level_two, lat_one, lat_two, classifier, labels, npix):
    lateral = project(level_one.astype(jnp.bfloat16), lat_one) + upsample(project(level_two.astype(jnp.bfloat16), lat_two))
    active, slope = gelu_pair(lateral)
    hidden = active.astype(jnp.bfloat16)
    logits = project(hidden, classifier)
    probs = jax.nn.softmax(logits, axis=-1)
    onehot = (labels[..., None] == jnp.arange(classifier.shape[1], dtype=jnp.int32)).astype(jnp.float32)
    grad_logits = (probs - onehot) * (loss_scale / npix)
    grad_lat = project_back(grad_logits.astype(jnp.bfloat16), classifier) * slope
    cot_one = project_back(grad_lat.astype(jnp.bfloat16), lat_one)
    cot_two = project_back(pool_sum(grad_lat).astype(jnp.bfloat16), lat_two)
    return cot_one, cot_two


def pad_crop(values):
    return jnp.pad(values, ((0, 0), (1, 1), (1, 1), (0, 0)))


def reference(stem, labels, up_proj, mix_proj, down_proj, dw_kernel, gain1, gain2, lat_one, lat_two, classifier):
    columns = up_proj.shape[0]
    crops, height, width, chan_one = stem.shape
    chan_two = up_proj.shape[1]
    state_one = jnp.zeros((crops, height, width, chan_one), jnp.float32)
    state_two = jnp.zeros((crops, height // 2, width // 2, chan_two), jnp.float32)
    stem_wide = stem.astype(jnp.float32)
    saves = []
    for column in range(columns):
        kernel = dw_kernel[column].astype(jnp.float32)
        narrow = state_two.astype(jnp.bfloat16)
        mixture = stem_wide + upsample(project(narrow, up_proj[column]))
        padded = pad_crop(mixture)
        depth = depthwise_apply(padded, kernel)
        active, slope_one = gelu_pair(depth)
        hidden = active.astype(jnp.bfloat16)
        state_one = gain1[column] * state_one + project(hidden, mix_proj[column])
        pooled = (pool_sum(state_one) * 0.25).astype(jnp.bfloat16)
        lifted, slope_two = gelu_pair(project(pooled, down_proj[column]))
        state_two = gain2[column] * state_two + lifted
        saves.append((narrow, padded, slope_one, hidden, pooled, slope_two))
    npix = float(crops * height * width)
    cot_one, cot_two = head_grads(state_one, state_two, lat_one, lat_two, classifier, labels, npix)
    grads_up = [None] * columns
    grads_mix = [None] * columns
    grads_down = [None] * columns
    grads_kernel = [None] * columns
    grad_stem = jnp.zeros(stem.shape, jnp.float32)
    for column in range(columns - 1, -1, -1):
        narrow, padded, slope_one, hidden, pooled, slope_two = saves[column]
        kernel = dw_kernel[column].astype(jnp.float32)
        grad_lift = (cot_two * slope_two).astype(jnp.bfloat16)
        grads_down[column] = outer_sum(pooled, grad_lift)
        total_one = cot_one + upsample(project_back(grad_lift, down_proj[column])) * 0.25
        total_narrow = total_one.astype(jnp.bfloat16)
        grads_mix[column] = outer_sum(hidden, total_narrow)
        grad_depth = project_back(total_narrow, mix_proj[column]) * slope_one
        grads_kernel[column] = kernel_terms(padded, grad_depth)
        grad_mixture = depthwise_adjoint(pad_crop(grad_depth), kernel)
        grad_stem = grad_stem + grad_mixture
        grad_narrow = pool_sum(grad_mixture).astype(jnp.bfloat16)
        grads_up[column] = outer_sum(narrow, grad_narrow)
        cot_two = gain2[column] * cot_two + project_back(grad_narrow, up_proj[column])
        cot_one = gain1[column] * total_one
    return (jnp.stack(grads_up, 0), jnp.stack(grads_mix, 0), jnp.stack(grads_down, 0), jnp.stack(grads_kernel, 0), grad_stem)
```

```python
import functools

import jax
import jax.numpy as jnp
from jax import lax
from jax.experimental import pallas as pl
from jax.experimental.pallas import tpu as pltpu
from jax.sharding import PartitionSpec as P

loss_scale = 64.0
root_coef = 0.7978845608028654
cube_coef = 0.044715
f32 = jnp.float32
bf16 = jnp.bfloat16
MESH = pl.DeviceIdType.MESH


def gelu_pair(values):
    square = values * values
    tangent = jnp.tanh(root_coef * (values + cube_coef * values * square))
    half = 0.5 * (1.0 + tangent)
    slope = half + 0.5 * values * (1.0 - tangent * tangent) * root_coef * (
        1.0 + 3.0 * cube_coef * square
    )
    return values * half, slope


def dot(left, right):
    return jnp.dot(left, right, preferred_element_type=f32)


def dot_back(left, right):
    return lax.dot_general(left, right, (((1,), (1,)), ((), ())), preferred_element_type=f32)


def dot_outer(left, right):
    return lax.dot_general(left, right, (((0,), (0,)), ((), ())), preferred_element_type=f32)


def up_to(count, multiple):
    return -(-count // multiple) * multiple


def spread(count, parts):
    run = count // parts
    padded = up_to(run, 16)
    source = lax.broadcasted_iota(jnp.int32, (count, 1), 0)
    target = source
    for part in range(1, parts):
        target = target + jnp.where(source >= part * run, padded - run, 0)
    spot = lax.broadcasted_iota(jnp.int32, (count, parts * padded), 1)
    return (spot == target).astype(f32).astype(bf16)


def pool_matrix(rows, width, axis_fine):
    fine, coarse = rows * width, rows * width // 4
    shape = (fine, coarse) if axis_fine == 0 else (coarse, fine)
    f = lax.broadcasted_iota(jnp.int32, shape, axis_fine)
    c = lax.broadcasted_iota(jnp.int32, shape, 1 - axis_fine)
    hit = jnp.zeros(shape, jnp.bool_)
    half = width // 2
    for row in range(rows // 2):
        rest = f - row * 2 * width
        inside = (rest >= 0) & (rest < 2 * width)
        rest = jnp.where(rest >= width, rest - width, rest)
        pos = 2 * (c - row * half)
        hit = hit | (inside & ((rest == pos) | (rest == pos + 1)))
    return hit.astype(f32).astype(bf16)


def kernel(
    S, D, T, M, rl, W, npix,
    stem, labels, up, mix, down, taps, gain1, gain2, lat1, lat2, cls,
    o_up, o_mix, o_down, o_taps, o_stem,
    stem_send, stem_full, lab_full, in1, in2, out1, out2, cin1, cin2, cout1, cout2,
    pad, mixture_s, slope1_s, hidden_s, narrow_s, pooled_s, slope2_s, total_s, lift_s, gnar_s,
    spread_u, spread_p, gs_send, gs_recv, acc_a, acc_d, gk, got_a, got_d, got_k,
    far_a, far_d, far_k,
    stem_ss, stem_rs, lab_ss, lab_rs, f_ss, f_rs, b_ss, b_rs, g_ss, g_rs,
    a_ss, a_rs, r_ss, r_rs,
):
    col, dp, strip = lax.axis_index("col"), lax.axis_index("dp"), lax.axis_index("strip")
    first, last = col == 0, col == S - 1
    C1, C2 = up.shape[1], up.shape[0]
    RW = rl * W
    pix = T * RW
    rows = T * rl
    wc = W // S
    par = lax.rem(dp, 2)
    mine = dp // 2
    Q = D // 2

    def remote(src, dst, ss, rs, target):
        return pltpu.make_async_remote_copy(
            src_ref=src, dst_ref=dst, send_sem=ss, recv_sem=rs,
            device_id=target, device_id_type=MESH,
        )

    def stem_copy(h, m, slot):
        return remote(
            stem_send.at[h, m], stem_full.at[m, slot], stem_ss.at[h, m], stem_rs.at[slot, m],
            {"strip": h},
        )

    def lab_copy(h, m, slot):
        return remote(
            labels.at[h * M + m], lab_full.at[m, slot], lab_ss.at[h, m], lab_rs.at[slot, m],
            {"strip": h},
        )

    for m in range(M):
        for h in range(T):
            stem_send[h, m] = stem[h * M + m].astype(f32)

            @pl.when(strip != h)
            def _():
                stem_copy(h, m, strip).start()
    for m in range(M):
        for h in range(T):

            @pl.when(strip != h)
            def _():
                lab_copy(h, m, strip).start()

            @pl.when(strip == h)
            def _():
                stem_full[m, h] = stem[h * M + m].astype(f32)
                lab_full[m, h] = labels[h * M + m]

    @pl.when(first)
    def _():
        in1[...] = jnp.zeros_like(in1)
        in2[...] = jnp.zeros_like(in2)

    pad[...] = jnp.zeros_like(pad)
    gk[...] = jnp.zeros_like(gk)
    kern = taps[0:9].astype(f32)
    g1 = gain1[...]
    g2 = gain2[...]
    spread_u[...] = pool_matrix(rows, W, 0)
    spread_p[...] = pool_matrix(rows, W, 1)
    place = lax.rem(lax.broadcasted_iota(jnp.int32, (pix, 1), 0), W)
    not_low = place != 0
    not_high = place != W - 1

    def widen(values):
        return dot(spread_u[...], values).astype(bf16)

    def pool(values):
        high = values.astype(bf16)
        low = (values - high.astype(f32)).astype(bf16)
        return dot(spread_p[...], high) + dot(spread_p[...], low)

    def sides(values):
        pad[8 : 8 + pix] = values
        before = jnp.where(not_low, pad[7 : 7 + pix], 0.0)
        after = jnp.where(not_high, pad[9 : 9 + pix], 0.0)
        return before, values, after

    def rows_moved(values, step):
        if step == 0:
            return values
        blank = jnp.zeros((W, values.shape[1]), f32)
        if step > 0:
            return jnp.concatenate([values[W:], blank], axis=0)
        return jnp.concatenate([blank, values[:-W]], axis=0)

    def depthwise(values, sign):
        trio = sides(values)
        total = None
        for i in (-1, 0, 1):
            line = None
            for j in (-1, 0, 1):
                t = 3 * (i + 1) + (j + 1)
                term = kern[t : t + 1] * trio[1 + sign * j]
                line = term if line is None else line + term
            line = rows_moved(line, sign * i)
            total = line if total is None else total + line
        return total

    def f_copy(n, m):
        src, dst = ((out1, in1), (out2, in2))[n]
        return remote(src.at[m], dst.at[m], f_ss.at[n, m], f_rs.at[n, m], {"col": col + 1})

    def b_copy(n, m):
        src, dst = ((cout1, cin1), (cout2, cin2))[n]
        return remote(src.at[m], dst.at[m], b_ss.at[n, m], b_rs.at[n, m], {"col": col - 1})

    def forward(m, carry):
        for h in range(T):

            @pl.when(strip != h)
            def _():
                stem_copy(h, m, h).wait_recv()

        @pl.when(jnp.logical_not(first))
        def _():
            f_copy(1, m).wait_recv()

        narrow = in2[m].astype(bf16)
        narrow_s[m] = narrow
        mixture = stem_full[m].reshape(pix, C1) + dot(widen(narrow), up[...])
        mixture_s[m] = mixture
        active, slope = gelu_pair(depthwise(mixture, 1))
        slope1_s[m] = slope
        hidden = active.astype(bf16)
        hidden_s[m] = hidden
        branch = dot(hidden, mix[...])

        @pl.when(jnp.logical_not(first))
        def _():
            f_copy(0, m).wait_recv()

        state1 = g1 * in1[m] + branch
        out1[m] = state1
        pooled = (pool(state1) * 0.25).astype(bf16)
        pooled_s[m] = pooled
        lifted, slope2 = gelu_pair(dot(pooled, down[...]))
        slope2_s[m] = slope2
        out2[m] = g2 * in2[m] + lifted

        @pl.when(jnp.logical_not(last))
        def _():
            f_copy(1, m).start()
            f_copy(0, m).start()

        return carry

    lax.fori_loop(0, M, forward, 0)

    def backward(m, carry):
        @pl.when(last)
        def _():
            for h in range(T):

                @pl.when(strip != h)
                def _():
                    lab_copy(h, m, h).wait_recv()

            lateral = dot(out1[m].astype(bf16), lat1[...]) + dot(
                widen(out2[m].astype(bf16)), lat2[...]
            )
            active, slope = gelu_pair(lateral)
            logits = dot(active.astype(bf16), cls[...])
            shifted = jnp.exp(logits - jnp.max(logits, axis=-1, keepdims=True))
            probs = shifted / jnp.sum(shifted, axis=-1, keepdims=True)
            label = lab_full[m].reshape(pix, 128)[:, 0:1]
            onehot = (lax.broadcasted_iota(jnp.int32, logits.shape, 1) == label).astype(f32)
            grad_logits = (probs - onehot) * (loss_scale / npix)
            grad_lat = dot_back(grad_logits.astype(bf16), cls[...]) * slope
            cin1[m] = dot_back(grad_lat.astype(bf16), lat1[...])
            cin2[m] = dot_back(pool(grad_lat).astype(bf16), lat2[...])

        @pl.when(jnp.logical_not(last))
        def _():
            b_copy(1, m).wait_recv()

        cot2 = cin2[m]
        lift = (cot2 * slope2_s[m]).astype(bf16)
        lift_s[m] = lift
        rise = dot_back(widen(lift), down[...]) * 0.25

        @pl.when(jnp.logical_not(last))
        def _():
            b_copy(0, m).wait_recv()

        total = cin1[m] + rise
        cout1[m] = g1 * total

        @pl.when(jnp.logical_not(first))
        def _():
            b_copy(0, m).start()

        total_narrow = total.astype(bf16)
        total_s[m] = total_narrow
        grad_depth = dot_back(total_narrow, mix[...]) * slope1_s[m]
        grad_mixture = depthwise(grad_depth, -1)
        grad_narrow = pool(grad_mixture).astype(bf16)
        gnar_s[m] = grad_narrow
        cout2[m] = g2 * cot2 + dot_back(grad_narrow, up[...])

        @pl.when(jnp.logical_not(first))
        def _():
            b_copy(1, m).start()

        cube = grad_mixture.reshape(rows, W, C1)
        for k in range(S):
            for h in range(T):
                gs_send[k, h, m] = cube[h * rl : (h + 1) * rl, k * wc : (k + 1) * wc]
        trio = sides(mixture_s[m])
        for i in (-1, 0, 1):
            for j in (-1, 0, 1):
                t = 3 * (i + 1) + (j + 1)
                window = rows_moved(trio[1 + j], i)
                gk[t : t + 1] += jnp.sum(window * grad_depth, axis=0, keepdims=True)
        return carry

    lax.fori_loop(0, M, backward, 0)

    def g_copy(k, h, sk, sh):
        return remote(
            gs_send.at[k, h], gs_recv.at[sk, sh], g_ss.at[k, h], g_rs.at[sk, sh],
            {"col": k, "strip": h},
        )

    for k in range(S):
        for h in range(T):
            other = (col != k) | (strip != h)

            @pl.when(other)
            def _():
                g_copy(k, h, col, strip).start()

            @pl.when(jnp.logical_not(other))
            def _():
                gs_recv[k, h] = gs_send[k, h]

    n = D * T
    flat = lambda ref: ref[...].reshape(-1, ref.shape[-1])
    pick1 = spread(C1, n)
    p1, p2 = up_to(C1 // n, 16), up_to(C2 // n, 16)
    pick2 = spread(C2, n)
    g_up = dot_outer(dot(flat(narrow_s), pick2).astype(bf16), flat(gnar_s))
    g_mix = dot_outer(dot(flat(hidden_s), pick1).astype(bf16), flat(total_s))
    g_down = dot_outer(dot(flat(pooled_s), pick1).astype(bf16), flat(lift_s))
    acc_a[:, :, :, 0:p2] = g_up.reshape(Q, 2, T, p2, C1)
    acc_a[:, :, :, p2:] = g_mix.reshape(Q, 2, T, p1, C1)
    acc_d[...] = g_down.reshape(Q, 2, T, p1, C2)

    partner = {"dp": dp + 1 - 2 * par}

    def a_copies(q):
        return (
            remote(acc_a.at[q, 1 - par], got_a.at[q], a_ss.at[q, 0], a_rs.at[q, 0], partner),
            remote(acc_d.at[q, 1 - par], got_d.at[q], a_ss.at[q, 1], a_rs.at[q, 1], partner),
        )

    k_copy = remote(gk, got_k, a_ss.at[Q, 0], a_rs.at[Q, 0], partner)
    for q in range(Q):
        for copy in a_copies(q):
            copy.start()
    k_copy.start()
    k_copy.wait_recv()
    k_copy.wait_send()
    gk[...] += got_k[...]

    def r_copies(q, h, sq, sh):
        target = {"dp": 2 * q + par, "strip": h}
        pairs = (
            (acc_a.at[q, par, h], far_a.at[sq, sh]),
            (acc_d.at[q, par, h], far_d.at[sq, sh]),
            (gk, far_k.at[sq, sh]),
        )
        return [
            remote(src, dst, r_ss.at[q, h, i], r_rs.at[sq, sh, i], target)
            for i, (src, dst) in enumerate(pairs)
        ]

    for q in range(Q):
        for copy in a_copies(q):
            copy.wait_recv()
        for h in range(T):
            acc_a[q, par, h] += got_a[q, h]
            acc_d[q, par, h] += got_d[q, h]
            other = (mine != q) | (strip != h)

            @pl.when(other)
            def _():
                for copy in r_copies(q, h, mine, strip):
                    copy.start()

            @pl.when(jnp.logical_not(other))
            def _():
                far_a[q, h] = acc_a[q, par, h]
                far_d[q, h] = acc_d[q, par, h]
                far_k[q, h] = gk[...]

    for k in range(S):
        for h in range(T):

            @pl.when((col != k) | (strip != h))
            def _():
                g_copy(k, h, k, h).wait_recv()

    for h in range(T):
        total = gs_recv[0, h]
        for k in range(1, S):
            total = total + gs_recv[k, h]
        o_stem[h * M : (h + 1) * M] = total

    for q in range(Q):
        for h in range(T):

            @pl.when((mine != q) | (strip != h))
            def _():
                for copy in r_copies(q, h, q, h):
                    copy.wait_recv()

    sum_a = sum_d = sum_k = 0.0
    for q in range(Q):
        for h in range(T):
            sum_a = sum_a + far_a[q, h]
            sum_d = sum_d + far_d[q, h]
            sum_k = sum_k + far_k[q, h]
    o_up[0] = sum_a[0 : C2 // n]
    o_mix[0] = sum_a[p2 : p2 + C1 // n]
    o_down[0] = sum_d[0 : C1 // n]
    o_taps[...] = sum_k

    for m in range(M):
        for h in range(T):

            @pl.when(strip != h)
            def _():
                stem_copy(h, m, strip).wait_send()
                lab_copy(h, m, strip).wait_send()

                @pl.when(jnp.logical_not(last))
                def _():
                    lab_copy(h, m, h).wait_recv()

        for i in range(2):

            @pl.when(jnp.logical_not(last))
            def _():
                f_copy(i, m).wait_send()

            @pl.when(jnp.logical_not(first))
            def _():
                b_copy(i, m).wait_send()

    for k in range(S):
        for h in range(T):

            @pl.when((col != k) | (strip != h))
            def _():
                g_copy(k, h, col, strip).wait_send()

    for q in range(Q):
        for copy in a_copies(q):
            copy.wait_send()
        for h in range(T):

            @pl.when((mine != q) | (strip != h))
            def _():
                for copy in r_copies(q, h, mine, strip):
                    copy.wait_send()


def shards(stem, labels, up, mix, down, taps, gain1, gain2, lat1, lat2, cls):
    B, rl, W, C1 = stem.shape
    C2 = up.shape[1]
    S, D, T = lax.axis_size("col"), lax.axis_size("dp"), lax.axis_size("strip")
    M = B // T
    RW = rl * W
    pix = T * RW
    small = pix // 4
    wc = W // S
    n = D * T
    Q = D // 2
    p1, p2 = up_to(C1 // n, 16), up_to(C2 // n, 16)
    npix = float(B * D * rl * T * W)
    lab = jnp.broadcast_to(labels.reshape(B, RW, 1), (B, RW, 128))
    V = pltpu.VMEM
    dma = pltpu.SemaphoreType.DMA
    vspec = pl.BlockSpec(memory_space=pltpu.VMEM)
    outs = pl.pallas_call(
        functools.partial(kernel, S, D, T, M, rl, W, npix),
        out_shape=(
            jax.ShapeDtypeStruct((1, C2 // n, C1), f32),
            jax.ShapeDtypeStruct((1, C1 // n, C1), f32),
            jax.ShapeDtypeStruct((1, C1 // n, C2), f32),
            jax.ShapeDtypeStruct((16, C1), f32),
            jax.ShapeDtypeStruct((B, rl, wc, C1), f32),
        ),
        in_specs=[vspec] * 11,
        out_specs=(vspec,) * 5,
        scratch_shapes=[
            V((T, M, RW, C1), f32),
            V((M, T, RW, C1), f32),
            V((M, T, RW, 128), jnp.int32),
            V((M, pix, C1), f32),
            V((M, small, C2), f32),
            V((M, pix, C1), f32),
            V((M, small, C2), f32),
            V((M, pix, C1), f32),
            V((M, small, C2), f32),
            V((M, pix, C1), f32),
            V((M, small, C2), f32),
            V((pix + 16, C1), f32),
            V((M, pix, C1), f32),
            V((M, pix, C1), f32),
            V((M, pix, C1), bf16),
            V((M, small, C2), bf16),
            V((M, small, C1), bf16),
            V((M, small, C2), f32),
            V((M, pix, C1), bf16),
            V((M, small, C2), bf16),
            V((M, small, C1), bf16),
            V((pix, small), bf16),
            V((small, pix), bf16),
            V((S, T, M, rl, wc, C1), f32),
            V((S, T, M, rl, wc, C1), f32),
            V((Q, 2, T, p1 + p2, C1), f32),
            V((Q, 2, T, p1, C2), f32),
            V((16, C1), f32),
            V((Q, T, p1 + p2, C1), f32),
            V((Q, T, p1, C2), f32),
            V((16, C1), f32),
            V((Q, T, p1 + p2, C1), f32),
            V((Q, T, p1, C2), f32),
            V((Q, T, 16, C1), f32),
            dma((T, M)),
            dma((T, M)),
            dma((T, M)),
            dma((T, M)),
            dma((2, M)),
            dma((2, M)),
            dma((2, M)),
            dma((2, M)),
            dma((S, T)),
            dma((S, T)),
            dma((Q + 1, 2)),
            dma((Q + 1, 2)),
            dma((Q, T, 3)),
            dma((Q, T, 3)),
        ],
        compiler_params=pltpu.CompilerParams(
            has_side_effects=True, vmem_limit_bytes=60000 * 1024
        ),
        name="columns",
    )(
        stem.reshape(B, RW, C1), lab, up[0], mix[0], down[0], taps[0], gain1, gain2,
        lat1, lat2, cls,
    )
    g_up, g_mix, g_down, g_taps, g_stem = outs
    index = lax.axis_index("dp") * T + lax.axis_index("strip")
    share = lax.dynamic_slice(g_taps, (0, index * (C1 // n)), (9, C1 // n))
    return g_up, g_mix, g_down, share[None], g_stem


def solution(mesh):
    placed = (
        P("dp", "strip", None, None),
        P("dp", "strip", None),
        P("col", None, None),
        P("col", None, None),
        P("col", None, None),
        P("col", None, None),
        P("col", None),
        P("col", None),
        P(),
        P(),
        P(),
    )
    return jax.shard_map(
        shards,
        mesh=mesh,
        in_specs=placed,
        out_specs=(
            P("col", ("dp", "strip"), None),
            P("col", ("dp", "strip"), None),
            P("col", ("dp", "strip"), None),
            P("col", None, ("dp", "strip")),
            P("dp", "strip", "col", None),
        ),
        check_vma=False,
    )
```

```python
import functools

import jax
import jax.numpy as jnp
from jax import lax
from jax.experimental import pallas as pl
from jax.experimental.pallas import tpu as pltpu
from jax.sharding import PartitionSpec as P

loss_scale = 64.0
root_coef = 0.7978845608028654
cube_coef = 0.044715
f32 = jnp.float32
bf16 = jnp.bfloat16
MESH = pl.DeviceIdType.MESH


def gelu_pair(values):
    square = values * values
    tangent = jnp.tanh(root_coef * (values + cube_coef * values * square))
    half = 0.5 * (1.0 + tangent)
    slope = half + 0.5 * values * (1.0 - tangent * tangent) * root_coef * (
        1.0 + 3.0 * cube_coef * square
    )
    return values * half, slope


def dot(left, right):
    return jnp.dot(left, right, preferred_element_type=f32)


def dot_back(left, right):
    return lax.dot_general(left, right, (((1,), (1,)), ((), ())), preferred_element_type=f32)


def dot_outer(left, right):
    return lax.dot_general(left, right, (((0,), (0,)), ((), ())), preferred_element_type=f32)


def up_to(count, multiple):
    return -(-count // multiple) * multiple


def spread(count, parts):
    run = count // parts
    padded = up_to(run, 16)
    source = lax.broadcasted_iota(jnp.int32, (count, 1), 0)
    target = source
    for part in range(1, parts):
        target = target + jnp.where(source >= part * run, padded - run, 0)
    spot = lax.broadcasted_iota(jnp.int32, (count, parts * padded), 1)
    return (spot == target).astype(f32).astype(bf16)


def pool_matrix(rows, width, axis_fine):
    fine, coarse = rows * width, rows * width // 4
    shape = (fine, coarse) if axis_fine == 0 else (coarse, fine)
    f = lax.broadcasted_iota(jnp.int32, shape, axis_fine)
    c = lax.broadcasted_iota(jnp.int32, shape, 1 - axis_fine)
    hit = jnp.zeros(shape, jnp.bool_)
    half = width // 2
    for row in range(rows // 2):
        rest = f - row * 2 * width
        inside = (rest >= 0) & (rest < 2 * width)
        rest = jnp.where(rest >= width, rest - width, rest)
        pos = 2 * (c - row * half)
        hit = hit | (inside & ((rest == pos) | (rest == pos + 1)))
    return hit.astype(f32).astype(bf16)


def kernel(
    S, D, T, M, rl, W, npix,
    stem, labels, up, mix, down, taps, gain1, gain2, lat1, lat2, cls,
    o_up, o_mix, o_down, o_taps, o_stem,
    stem_send, stem_full, lab_full, in1, in2, out1, out2, cin1, cin2, cout1, cout2,
    inp, outp, cinp, coutp, branch_s,
    pad, mixture_s, slope1_s, hidden_s, narrow_s, pooled_s, slope2_s, total_s, lift_s, gnar_s,
    spread_u, spread_p, gs_send, gs_recv, acc_a, acc_d, gk, got_a, got_d, got_k,
    far_a, far_d, far_k,
    stem_ss, stem_rs, lab_ss, lab_rs, f_ss, f_rs, b_ss, b_rs, g_ss, g_rs,
    a_ss, a_rs, r_ss, r_rs,
):
    col, dp, strip = lax.axis_index("col"), lax.axis_index("dp"), lax.axis_index("strip")
    first, last = col == 0, col == S - 1
    C1, C2 = up.shape[1], up.shape[0]
    RW = rl * W
    pix = T * RW
    rows = T * rl
    wc = W // S
    par = lax.rem(dp, 2)
    mine = dp // 2
    Q = D // 2

    def remote(src, dst, ss, rs, target):
        return pltpu.make_async_remote_copy(
            src_ref=src, dst_ref=dst, send_sem=ss, recv_sem=rs,
            device_id=target, device_id_type=MESH,
        )

    def stem_copy(h, m, slot):
        return remote(
            stem_send.at[h, m], stem_full.at[m, slot], stem_ss.at[h, m], stem_rs.at[slot, m],
            {"strip": h},
        )

    def lab_copy(h, m, slot):
        return remote(
            labels.at[h * M + m], lab_full.at[m, slot], lab_ss.at[h, m], lab_rs.at[slot, m],
            {"strip": h},
        )

    for m in range(M):
        for h in range(T):
            stem_send[h, m] = stem[h * M + m].astype(f32)

            @pl.when(strip != h)
            def _():
                stem_copy(h, m, strip).start()
    for m in range(M):
        for h in range(T):

            @pl.when(strip != h)
            def _():
                lab_copy(h, m, strip).start()

            @pl.when(strip == h)
            def _():
                stem_full[m, h] = stem[h * M + m].astype(f32)
                lab_full[m, h] = labels[h * M + m]

    @pl.when(first)
    def _():
        in1[...] = jnp.zeros_like(in1)
        in2[...] = jnp.zeros_like(in2)
        inp[...] = jnp.zeros_like(inp)

    @pl.when(last)
    def _():
        cinp[...] = jnp.zeros_like(cinp)

    pad[...] = jnp.zeros_like(pad)
    gk[...] = jnp.zeros_like(gk)
    kern = taps[0:9].astype(f32)
    g1 = gain1[...]
    g2 = gain2[...]
    spread_u[...] = pool_matrix(rows, W, 0)
    spread_p[...] = pool_matrix(rows, W, 1)
    place = lax.rem(lax.broadcasted_iota(jnp.int32, (pix, 1), 0), W)
    not_low = place != 0
    not_high = place != W - 1

    def widen(values):
        return dot(spread_u[...], values).astype(bf16)

    def pool(values):
        high = values.astype(bf16)
        low = (values - high.astype(f32)).astype(bf16)
        return dot(spread_p[...], high) + dot(spread_p[...], low)

    def sides(values):
        pad[8 : 8 + pix] = values
        before = jnp.where(not_low, pad[7 : 7 + pix], 0.0)
        after = jnp.where(not_high, pad[9 : 9 + pix], 0.0)
        return before, values, after

    def rows_moved(values, step):
        if step == 0:
            return values
        blank = jnp.zeros((W, values.shape[1]), f32)
        if step > 0:
            return jnp.concatenate([values[W:], blank], axis=0)
        return jnp.concatenate([blank, values[:-W]], axis=0)

    def depthwise(values, sign):
        trio = sides(values)
        total = None
        for i in (-1, 0, 1):
            line = None
            for j in (-1, 0, 1):
                t = 3 * (i + 1) + (j + 1)
                term = kern[t : t + 1] * trio[1 + sign * j]
                line = term if line is None else line + term
            line = rows_moved(line, sign * i)
            total = line if total is None else total + line
        return total

    def f_copy(n, m):
        src, dst = ((out1, in1), (out2, in2), (outp, inp))[n]
        return remote(src.at[m], dst.at[m], f_ss.at[n, m], f_rs.at[n, m], {"col": col + 1})

    def b_copy(n, m):
        src, dst = ((cout1, cin1), (cout2, cin2), (coutp, cinp))[n]
        return remote(src.at[m], dst.at[m], b_ss.at[n, m], b_rs.at[n, m], {"col": col - 1})

    def forward(m, carry):
        for h in range(T):

            @pl.when(strip != h)
            def _():
                stem_copy(h, m, h).wait_recv()

        @pl.when(jnp.logical_not(first))
        def _():
            f_copy(1, m).wait_recv()

        narrow = in2[m].astype(bf16)
        narrow_s[m] = narrow
        mixture = stem_full[m].reshape(pix, C1) + dot(widen(narrow), up[...])
        mixture_s[m] = mixture
        active, slope = gelu_pair(depthwise(mixture, 1))
        slope1_s[m] = slope
        hidden = active.astype(bf16)
        hidden_s[m] = hidden
        branch = dot(hidden, mix[...])
        branch_s[m] = branch
        pool_branch = pool(branch)

        @pl.when(jnp.logical_not(first))
        def _():
            f_copy(2, m).wait_recv()

        low1 = g1 * inp[m] + pool_branch
        outp[m] = low1
        pooled = (low1 * 0.25).astype(bf16)
        pooled_s[m] = pooled
        lifted, slope2 = gelu_pair(dot(pooled, down[...]))
        slope2_s[m] = slope2
        out2[m] = g2 * in2[m] + lifted

        @pl.when(jnp.logical_not(last))
        def _():
            f_copy(1, m).start()
            f_copy(2, m).start()

        return carry

    lax.fori_loop(0, M, forward, 0)

    def full_state(m):
        @pl.when(jnp.logical_not(first))
        def _():
            f_copy(0, m).wait_recv()

        out1[m] = g1 * in1[m] + branch_s[m]

        @pl.when(jnp.logical_not(last))
        def _():
            f_copy(0, m).start()

    def backward(m, carry):
        @pl.when(last)
        def _():
            full_state(m)
            for h in range(T):

                @pl.when(strip != h)
                def _():
                    lab_copy(h, m, h).wait_recv()

            lateral = dot(out1[m].astype(bf16), lat1[...]) + dot(
                widen(out2[m].astype(bf16)), lat2[...]
            )
            active, slope = gelu_pair(lateral)
            logits = dot_back(active.astype(bf16), cls[...])
            shifted = jnp.exp(logits - jnp.max(logits, axis=-1, keepdims=True))
            probs = shifted / jnp.sum(shifted, axis=-1, keepdims=True)
            eye = lax.broadcasted_iota(jnp.int32, (W, W), 0) == lax.broadcasted_iota(
                jnp.int32, (W, W), 1
            )
            lines = []
            for h in range(T):
                block = lab_full[m, h].astype(f32)
                for r in range(rl):
                    turned = jnp.where(eye, block[r : r + 1], 0.0)
                    lines.append(jnp.sum(turned, axis=1, keepdims=True))
            label = jnp.concatenate(lines, axis=0).astype(jnp.int32)
            onehot = (lax.broadcasted_iota(jnp.int32, logits.shape, 1) == label).astype(f32)
            grad_logits = (probs - onehot) * (loss_scale / npix)
            grad_lat = dot(grad_logits.astype(bf16), cls[...]) * slope
            cin1[m] = dot_back(grad_lat.astype(bf16), lat1[...])
            cin2[m] = dot_back(pool(grad_lat).astype(bf16), lat2[...])

        @pl.when(jnp.logical_not(last))
        def _():
            b_copy(0, m).wait_recv()

        @pl.when(jnp.logical_not(first))
        def _():
            cout1[m] = g1 * cin1[m]
            b_copy(0, m).start()

        @pl.when(jnp.logical_not(last))
        def _():
            b_copy(1, m).wait_recv()

        cot2 = cin2[m]
        lift = (cot2 * slope2_s[m]).astype(bf16)
        lift_s[m] = lift
        rise = dot_back(lift, down[...]) * 0.25

        @pl.when(jnp.logical_not(last))
        def _():
            b_copy(2, m).wait_recv()

        rise = cinp[m] + rise

        @pl.when(jnp.logical_not(first))
        def _():
            coutp[m] = g1 * rise
            b_copy(2, m).start()

        high = rise.astype(bf16)
        low = (rise - high.astype(f32)).astype(bf16)
        total = cin1[m] + (dot(spread_u[...], high) + dot(spread_u[...], low))
        total_narrow = total.astype(bf16)
        total_s[m] = total_narrow
        grad_depth = dot_back(total_narrow, mix[...]) * slope1_s[m]
        grad_mixture = depthwise(grad_depth, -1)
        grad_narrow = pool(grad_mixture).astype(bf16)
        gnar_s[m] = grad_narrow
        cout2[m] = g2 * cot2 + dot_back(grad_narrow, up[...])

        @pl.when(jnp.logical_not(first))
        def _():
            b_copy(1, m).start()

        cube = grad_mixture.reshape(rows, W, C1)
        for k in range(S):
            for h in range(T):
                gs_send[k, h, m] = cube[h * rl : (h + 1) * rl, k * wc : (k + 1) * wc]
        trio = sides(mixture_s[m])
        for i in (-1, 0, 1):
            for j in (-1, 0, 1):
                t = 3 * (i + 1) + (j + 1)
                window = rows_moved(trio[1 + j], i)
                gk[t : t + 1] += jnp.sum(window * grad_depth, axis=0, keepdims=True)
        return carry

    @pl.when(jnp.logical_not(last))
    def _():
        for m in range(M):
            full_state(m)

    lax.fori_loop(0, M, backward, 0)

    def g_copy(k, h, sk, sh):
        return remote(
            gs_send.at[k, h], gs_recv.at[sk, sh], g_ss.at[k, h], g_rs.at[sk, sh],
            {"col": k, "strip": h},
        )

    for k in range(S):
        for h in range(T):
            other = (col != k) | (strip != h)

            @pl.when(other)
            def _():
                g_copy(k, h, col, strip).start()

            @pl.when(jnp.logical_not(other))
            def _():
                gs_recv[k, h] = gs_send[k, h]

    n = D * T
    flat = lambda ref: ref[...].reshape(-1, ref.shape[-1])
    pick1 = spread(C1, n)
    p1, p2 = up_to(C1 // n, 16), up_to(C2 // n, 16)
    pick2 = spread(C2, n)
    g_up = dot_outer(dot(flat(narrow_s), pick2).astype(bf16), flat(gnar_s))
    g_mix = dot_outer(dot(flat(hidden_s), pick1).astype(bf16), flat(total_s))
    g_down = dot_outer(dot(flat(pooled_s), pick1).astype(bf16), flat(lift_s))
    acc_a[:, :, :, 0:p2] = g_up.reshape(Q, 2, T, p2, C1)
    acc_a[:, :, :, p2:] = g_mix.reshape(Q, 2, T, p1, C1)
    acc_d[...] = g_down.reshape(Q, 2, T, p1, C2)

    partner = {"dp": dp + 1 - 2 * par}

    def a_copies(q):
        return (
            remote(acc_a.at[q, 1 - par], got_a.at[q], a_ss.at[q, 0], a_rs.at[q, 0], partner),
            remote(acc_d.at[q, 1 - par], got_d.at[q], a_ss.at[q, 1], a_rs.at[q, 1], partner),
        )

    k_copy = remote(gk, got_k, a_ss.at[Q, 0], a_rs.at[Q, 0], partner)
    for q in range(Q):
        for copy in a_copies(q):
            copy.start()
    k_copy.start()
    k_copy.wait_recv()
    k_copy.wait_send()
    gk[...] += got_k[...]

    def r_copies(q, h, sq, sh):
        target = {"dp": 2 * q + par, "strip": h}
        pairs = (
            (acc_a.at[q, par, h], far_a.at[sq, sh]),
            (acc_d.at[q, par, h], far_d.at[sq, sh]),
            (gk, far_k.at[sq, sh]),
        )
        return [
            remote(src, dst, r_ss.at[q, h, i], r_rs.at[sq, sh, i], target)
            for i, (src, dst) in enumerate(pairs)
        ]

    for q in range(Q):
        for copy in a_copies(q):
            copy.wait_recv()
        for h in range(T):
            acc_a[q, par, h] += got_a[q, h]
            acc_d[q, par, h] += got_d[q, h]
            other = (mine != q) | (strip != h)

            @pl.when(other)
            def _():
                for copy in r_copies(q, h, mine, strip):
                    copy.start()

            @pl.when(jnp.logical_not(other))
            def _():
                far_a[q, h] = acc_a[q, par, h]
                far_d[q, h] = acc_d[q, par, h]
                far_k[q, h] = gk[...]

    for k in range(S):
        for h in range(T):

            @pl.when((col != k) | (strip != h))
            def _():
                g_copy(k, h, k, h).wait_recv()

    for h in range(T):
        total = gs_recv[0, h]
        for k in range(1, S):
            total = total + gs_recv[k, h]
        o_stem[h * M : (h + 1) * M] = total

    for q in range(Q):
        for h in range(T):

            @pl.when((mine != q) | (strip != h))
            def _():
                for copy in r_copies(q, h, q, h):
                    copy.wait_recv()

    sum_a = sum_d = sum_k = 0.0
    for q in range(Q):
        for h in range(T):
            sum_a = sum_a + far_a[q, h]
            sum_d = sum_d + far_d[q, h]
            sum_k = sum_k + far_k[q, h]
    o_up[...] = sum_a[0 : C2 // n]
    o_mix[...] = sum_a[p2 : p2 + C1 // n]
    o_down[...] = sum_d[0 : C1 // n]
    w = C1 // n
    share = sum_k[0:9, 0:w]
    for k in range(1, n):
        share = jnp.where(dp * T + strip == k, sum_k[0:9, k * w : (k + 1) * w], share)
    o_taps[...] = share

    for m in range(M):
        for h in range(T):

            @pl.when(strip != h)
            def _():
                stem_copy(h, m, strip).wait_send()
                lab_copy(h, m, strip).wait_send()

                @pl.when(jnp.logical_not(last))
                def _():
                    lab_copy(h, m, h).wait_recv()

        for i in range(3):

            @pl.when(jnp.logical_not(last))
            def _():
                f_copy(i, m).wait_send()

            @pl.when(jnp.logical_not(first))
            def _():
                b_copy(i, m).wait_send()

    for k in range(S):
        for h in range(T):

            @pl.when((col != k) | (strip != h))
            def _():
                g_copy(k, h, col, strip).wait_send()

    for q in range(Q):
        for copy in a_copies(q):
            copy.wait_send()
        for h in range(T):

            @pl.when((mine != q) | (strip != h))
            def _():
                for copy in r_copies(q, h, mine, strip):
                    copy.wait_send()


def finish(*refs):
    for source, target in zip(refs[:4], refs[5:9]):
        target[...] = source[...].reshape(target.shape)
    refs[9][...] = refs[4][...]


def shards(stem, labels, up, mix, down, taps, gain1, gain2, lat1, lat2, cls):
    B, rl, W, C1 = stem.shape
    C2 = up.shape[1]
    S, D, T = lax.axis_size("col"), lax.axis_size("dp"), lax.axis_size("strip")
    M = B // T
    RW = rl * W
    pix = T * RW
    small = pix // 4
    wc = W // S
    n = D * T
    Q = D // 2
    p1, p2 = up_to(C1 // n, 16), up_to(C2 // n, 16)
    npix = float(B * D * rl * T * W)
    V = pltpu.VMEM
    dma = pltpu.SemaphoreType.DMA
    vspec = pl.BlockSpec(memory_space=pltpu.VMEM)
    outs = pl.pallas_call(
        functools.partial(kernel, S, D, T, M, rl, W, npix),
        out_shape=(
            jax.ShapeDtypeStruct((C2 // n, C1), f32),
            jax.ShapeDtypeStruct((C1 // n, C1), f32),
            jax.ShapeDtypeStruct((C1 // n, C2), f32),
            jax.ShapeDtypeStruct((9, C1 // n), f32),
            jax.ShapeDtypeStruct((B, rl, wc, C1), f32),
        ),
        in_specs=[vspec] * 11,
        out_specs=(vspec,) * 5,
        scratch_shapes=[
            V((T, M, RW, C1), f32),
            V((M, T, RW, C1), f32),
            V((M, T, rl, W), jnp.int32),
            V((M, pix, C1), f32),
            V((M, small, C2), f32),
            V((M, pix, C1), f32),
            V((M, small, C2), f32),
            V((M, pix, C1), f32),
            V((M, small, C2), f32),
            V((M, pix, C1), f32),
            V((M, small, C2), f32),
            V((M, small, C1), f32),
            V((M, small, C1), f32),
            V((M, small, C1), f32),
            V((M, small, C1), f32),
            V((M, pix, C1), f32),
            V((pix + 16, C1), f32),
            V((M, pix, C1), f32),
            V((M, pix, C1), f32),
            V((M, pix, C1), bf16),
            V((M, small, C2), bf16),
            V((M, small, C1), bf16),
            V((M, small, C2), f32),
            V((M, pix, C1), bf16),
            V((M, small, C2), bf16),
            V((M, small, C1), bf16),
            V((pix, small), bf16),
            V((small, pix), bf16),
            V((S, T, M, rl, wc, C1), f32),
            V((S, T, M, rl, wc, C1), f32),
            V((Q, 2, T, p1 + p2, C1), f32),
            V((Q, 2, T, p1, C2), f32),
            V((16, C1), f32),
            V((Q, T, p1 + p2, C1), f32),
            V((Q, T, p1, C2), f32),
            V((16, C1), f32),
            V((Q, T, p1 + p2, C1), f32),
            V((Q, T, p1, C2), f32),
            V((Q, T, 16, C1), f32),
            dma((T, M)),
            dma((T, M)),
            dma((T, M)),
            dma((T, M)),
            dma((3, M)),
            dma((3, M)),
            dma((3, M)),
            dma((3, M)),
            dma((S, T)),
            dma((S, T)),
            dma((Q + 1, 2)),
            dma((Q + 1, 2)),
            dma((Q, T, 3)),
            dma((Q, T, 3)),
        ],
        compiler_params=pltpu.CompilerParams(
            has_side_effects=True, vmem_limit_bytes=60000 * 1024
        ),
        name="columns",
    )(
        stem.reshape(B, RW, C1), labels, up[0], mix[0], down[0], taps[0], gain1, gain2,
        lat1, lat2, cls.T,
    )
    tall = lambda a: jax.ShapeDtypeStruct((a.shape[0], 1, a.shape[1]), f32)
    done = pl.pallas_call(
        finish,
        out_shape=tuple(tall(a) for a in outs[:4])
        + (jax.ShapeDtypeStruct(outs[4].shape, f32),),
        in_specs=[vspec] * 5,
        out_specs=(vspec,) * 5,
        name="finish",
    )(*outs)
    return tuple(jnp.transpose(a, (1, 0, 2)) for a in done[:4]) + (done[4],)


def solution(mesh):
    placed = (
        P("dp", "strip", None, None),
        P("dp", "strip", None),
        P("col", None, None),
        P("col", None, None),
        P("col", None, None),
        P("col", None, None),
        P("col", None),
        P("col", None),
        P(),
        P(),
        P(),
    )
    return jax.shard_map(
        shards,
        mesh=mesh,
        in_specs=placed,
        out_specs=(
            P("col", ("dp", "strip"), None),
            P("col", ("dp", "strip"), None),
            P("col", ("dp", "strip"), None),
            P("col", None, ("dp", "strip")),
            P("dp", "strip", "col", None),
        ),
        check_vma=False,
    )
```

```python
import functools

import jax
import jax.numpy as jnp
from jax import lax
from jax.experimental import pallas as pl
from jax.experimental.pallas import tpu as pltpu
from jax.sharding import PartitionSpec as P

loss_scale = 64.0
root_coef = 0.7978845608028654
cube_coef = 0.044715
f32 = jnp.float32
bf16 = jnp.bfloat16
MESH = pl.DeviceIdType.MESH


def gelu_pair(values):
    square = values * values
    tangent = jnp.tanh(root_coef * (values + cube_coef * values * square))
    half = 0.5 * (1.0 + tangent)
    slope = half + 0.5 * values * (1.0 - tangent * tangent) * root_coef * (
        1.0 + 3.0 * cube_coef * square
    )
    return values * half, slope


def dot(left, right):
    return jnp.dot(left, right, preferred_element_type=f32)


def dot_back(left, right):
    return lax.dot_general(left, right, (((1,), (1,)), ((), ())), preferred_element_type=f32)


def dot_outer(left, right):
    return lax.dot_general(left, right, (((0,), (0,)), ((), ())), preferred_element_type=f32)


def up_to(count, multiple):
    return -(-count // multiple) * multiple


def spread(count, parts):
    run = count // parts
    padded = up_to(run, 16)
    source = lax.broadcasted_iota(jnp.int32, (count, 1), 0)
    target = source
    for part in range(1, parts):
        target = target + jnp.where(source >= part * run, padded - run, 0)
    spot = lax.broadcasted_iota(jnp.int32, (count, parts * padded), 1)
    return (spot == target).astype(f32).astype(bf16)


def pool_matrix(rows, width, axis_fine):
    fine, coarse = rows * width, rows * width // 4
    shape = (fine, coarse) if axis_fine == 0 else (coarse, fine)
    f = lax.broadcasted_iota(jnp.int32, shape, axis_fine)
    c = lax.broadcasted_iota(jnp.int32, shape, 1 - axis_fine)
    hit = jnp.zeros(shape, jnp.bool_)
    half = width // 2
    for row in range(rows // 2):
        rest = f - row * 2 * width
        inside = (rest >= 0) & (rest < 2 * width)
        rest = jnp.where(rest >= width, rest - width, rest)
        pos = 2 * (c - row * half)
        hit = hit | (inside & ((rest == pos) | (rest == pos + 1)))
    return hit.astype(f32).astype(bf16)


def kernel(
    S, D, T, M, rl, W, npix,
    stem, labels, up, mix, down, taps, gain1, gain2, lat1, lat2, cls,
    o_up, o_mix, o_down, o_taps, o_stem,
    stem_send, stem_full, lab_full, in1, in2, out1, out2, cin1, cin2, cout1, cout2,
    inp, outp, cinp, coutp, branch_s, hidden_c, pooled_c, narrow_c,
    pad, mixture_s, slope1_s, hidden_s, narrow_s, pooled_s, slope2_s, total_s, lift_s, gnar_s,
    spread_u, spread_p, gs_send, gs_recv, acc_a, acc_d, gk, got_a, got_d, got_k,
    far_a, far_d, far_k,
    stem_ss, stem_rs, lab_ss, lab_rs, f_ss, f_rs, b_ss, b_rs, g_ss, g_rs,
    a_ss, a_rs, r_ss, r_rs,
):
    col, dp, strip = lax.axis_index("col"), lax.axis_index("dp"), lax.axis_index("strip")
    first, last = col == 0, col == S - 1
    C1, C2 = up.shape[1], up.shape[0]
    RW = rl * W
    pix = T * RW
    rows = T * rl
    wc = W // S
    par = lax.rem(dp, 2)
    mine = dp // 2
    Q = D // 2

    def remote(src, dst, ss, rs, target):
        return pltpu.make_async_remote_copy(
            src_ref=src, dst_ref=dst, send_sem=ss, recv_sem=rs,
            device_id=target, device_id_type=MESH,
        )

    gate = pltpu.get_barrier_semaphore()
    for h in range(T):
        for k in range(S):

            @pl.when((col != k) | (strip != h))
            def _():
                pl.semaphore_signal(
                    gate, inc=1, device_id={"col": k, "strip": h}, device_id_type=MESH
                )

        for d in range(D):

            @pl.when(dp != d)
            def _():
                pl.semaphore_signal(
                    gate, inc=1, device_id={"dp": d, "strip": h}, device_id_type=MESH
                )

    for m in range(M):
        for h in range(T):
            stem_send[h, m] = stem[h * M + m].astype(f32)

    @pl.when(first)
    def _():
        in1[...] = jnp.zeros_like(in1)
        in2[...] = jnp.zeros_like(in2)
        inp[...] = jnp.zeros_like(inp)

    @pl.when(last)
    def _():
        cinp[...] = jnp.zeros_like(cinp)

    pad[...] = jnp.zeros_like(pad)
    gk[...] = jnp.zeros_like(gk)
    spread_u[...] = pool_matrix(rows, W, 0)
    spread_p[...] = pool_matrix(rows, W, 1)
    pl.semaphore_wait(gate, S * T - 1 + (D - 1) * T)

    def stem_copy(h, m, slot):
        return remote(
            stem_send.at[h, m], stem_full.at[m, slot], stem_ss.at[h, m], stem_rs.at[slot, m],
            {"strip": h},
        )

    def lab_copy(h, m, slot):
        return remote(
            labels.at[h * M + m], lab_full.at[m, slot], lab_ss.at[h, m], lab_rs.at[slot, m],
            {"strip": h},
        )

    for m in range(M):
        for h in range(T):
            @pl.when(strip != h)
            def _():
                stem_copy(h, m, strip).start()
    for m in range(M):
        for h in range(T):

            @pl.when(strip != h)
            def _():
                lab_copy(h, m, strip).start()

            @pl.when(strip == h)
            def _():
                stem_full[m, h] = stem[h * M + m].astype(f32)
                lab_full[m, h] = labels[h * M + m]

    kern = taps[0:9].astype(f32)
    g1 = gain1[...]
    g2 = gain2[...]
    place = lax.rem(lax.broadcasted_iota(jnp.int32, (pix, 1), 0), W)
    not_low = place != 0
    not_high = place != W - 1

    def widen(values):
        return dot(spread_u[...], values).astype(bf16)

    def pool(values):
        high = values.astype(bf16)
        low = (values - high.astype(f32)).astype(bf16)
        return dot(spread_p[...], high) + dot(spread_p[...], low)

    def sides(values):
        pad[8 : 8 + pix] = values
        before = jnp.where(not_low, pad[7 : 7 + pix], 0.0)
        after = jnp.where(not_high, pad[9 : 9 + pix], 0.0)
        return before, values, after

    def rows_moved(values, step):
        if step == 0:
            return values
        blank = jnp.zeros((W, values.shape[1]), f32)
        if step > 0:
            return jnp.concatenate([values[W:], blank], axis=0)
        return jnp.concatenate([blank, values[:-W]], axis=0)

    def depthwise(values, sign):
        trio = sides(values)
        total = None
        for i in (-1, 0, 1):
            line = None
            for j in (-1, 0, 1):
                t = 3 * (i + 1) + (j + 1)
                term = kern[t : t + 1] * trio[1 + sign * j]
                line = term if line is None else line + term
            line = rows_moved(line, sign * i)
            total = line if total is None else total + line
        return total

    def f_copy(n, m):
        src, dst = ((out1, in1), (out2, in2), (outp, inp))[n]
        return remote(src.at[m], dst.at[m], f_ss.at[n, m], f_rs.at[n, m], {"col": col + 1})

    def b_copy(n, m):
        src, dst = ((cout1, cin1), (cout2, cin2), (coutp, cinp))[n]
        return remote(src.at[m], dst.at[m], b_ss.at[n, m], b_rs.at[n, m], {"col": col - 1})

    def forward(m, carry):
        for h in range(T):

            @pl.when(strip != h)
            def _():
                stem_copy(h, m, h).wait_recv()

        @pl.when(jnp.logical_not(first))
        def _():
            f_copy(1, m).wait_recv()

        narrow = in2[m].astype(bf16)
        narrow_s[m] = narrow
        mixture = stem_full[m].reshape(pix, C1) + dot(widen(narrow), up[...])
        mixture_s[m] = mixture
        active, slope = gelu_pair(depthwise(mixture, 1))
        slope1_s[m] = slope
        hidden = active.astype(bf16)
        hidden_s[m] = hidden
        branch = dot(hidden, mix[...])
        branch_s[m] = branch
        pool_branch = pool(branch)

        @pl.when(jnp.logical_not(first))
        def _():
            f_copy(2, m).wait_recv()

        low1 = g1 * inp[m] + pool_branch
        outp[m] = low1
        pooled = (low1 * 0.25).astype(bf16)
        pooled_s[m] = pooled
        lifted, slope2 = gelu_pair(dot(pooled, down[...]))
        slope2_s[m] = slope2
        out2[m] = g2 * in2[m] + lifted

        @pl.when(jnp.logical_not(last))
        def _():
            f_copy(1, m).start()
            f_copy(2, m).start()

        return carry

    lax.fori_loop(0, M, forward, 0)

    def full_state(m):
        @pl.when(jnp.logical_not(first))
        def _():
            f_copy(0, m).wait_recv()

        out1[m] = g1 * in1[m] + branch_s[m]

        @pl.when(jnp.logical_not(last))
        def _():
            f_copy(0, m).start()

    def g_copy(k, h, m, sk, sh):
        return remote(
            gs_send.at[k, h, m], gs_recv.at[sk, sh, m], g_ss.at[k, h, m], g_rs.at[sk, sh, m],
            {"col": k, "strip": h},
        )

    def stem_out(m, carry):
        for k in range(S):
            for h in range(T):
                other = (col != k) | (strip != h)

                @pl.when(other)
                def _():
                    g_copy(k, h, m, col, strip).start()

                @pl.when(jnp.logical_not(other))
                def _():
                    gs_recv[k, h, m] = gs_send[k, h, m]

        return carry

    def backward(m, carry):
        @pl.when(last)
        def _():
            full_state(m)
            for h in range(T):

                @pl.when(strip != h)
                def _():
                    lab_copy(h, m, h).wait_recv()

            lateral = dot(out1[m].astype(bf16), lat1[...]) + dot(
                widen(out2[m].astype(bf16)), lat2[...]
            )
            active, slope = gelu_pair(lateral)
            logits = dot_back(active.astype(bf16), cls[...])
            shifted = jnp.exp(logits - jnp.max(logits, axis=-1, keepdims=True))
            probs = shifted / jnp.sum(shifted, axis=-1, keepdims=True)
            eye = lax.broadcasted_iota(jnp.int32, (W, W), 0) == lax.broadcasted_iota(
                jnp.int32, (W, W), 1
            )
            lines = []
            for h in range(T):
                block = lab_full[m, h].astype(f32)
                for r in range(rl):
                    turned = jnp.where(eye, block[r : r + 1], 0.0)
                    lines.append(jnp.sum(turned, axis=1, keepdims=True))
            label = jnp.concatenate(lines, axis=0).astype(jnp.int32)
            onehot = (lax.broadcasted_iota(jnp.int32, logits.shape, 1) == label).astype(f32)
            grad_logits = (probs - onehot) * (loss_scale / npix)
            grad_lat = dot(grad_logits.astype(bf16), cls[...]) * slope
            cin1[m] = dot_back(grad_lat.astype(bf16), lat1[...])
            cin2[m] = dot_back(pool(grad_lat).astype(bf16), lat2[...])

        @pl.when(jnp.logical_not(last))
        def _():
            b_copy(0, m).wait_recv()

        @pl.when(jnp.logical_not(first))
        def _():
            cout1[m] = g1 * cin1[m]
            b_copy(0, m).start()

        @pl.when(jnp.logical_not(last))
        def _():
            b_copy(1, m).wait_recv()

        cot2 = cin2[m]
        lift = (cot2 * slope2_s[m]).astype(bf16)
        lift_s[m] = lift
        rise = dot_back(lift, down[...]) * 0.25

        @pl.when(jnp.logical_not(last))
        def _():
            b_copy(2, m).wait_recv()

        rise = cinp[m] + rise

        @pl.when(jnp.logical_not(first))
        def _():
            coutp[m] = g1 * rise
            b_copy(2, m).start()

        high = rise.astype(bf16)
        low = (rise - high.astype(f32)).astype(bf16)
        total = cin1[m] + (dot(spread_u[...], high) + dot(spread_u[...], low))
        total_narrow = total.astype(bf16)
        total_s[m] = total_narrow
        grad_depth = dot_back(total_narrow, mix[...]) * slope1_s[m]
        grad_mixture = depthwise(grad_depth, -1)
        grad_narrow = pool(grad_mixture).astype(bf16)
        gnar_s[m] = grad_narrow
        cout2[m] = g2 * cot2 + dot_back(grad_narrow, up[...])

        @pl.when(jnp.logical_not(first))
        def _():
            b_copy(1, m).start()

        cube = grad_mixture.reshape(rows, W, C1)
        for k in range(S):
            for h in range(T):
                gs_send[k, h, m] = cube[h * rl : (h + 1) * rl, k * wc : (k + 1) * wc]
        @pl.when(first)
        def _():
            stem_out(m, 0)

        trio = sides(mixture_s[m])
        for i in (-1, 0, 1):
            for j in (-1, 0, 1):
                t = 3 * (i + 1) + (j + 1)
                window = rows_moved(trio[1 + j], i)
                gk[t : t + 1] += jnp.sum(window * grad_depth, axis=0, keepdims=True)
        return carry

    n = D * T
    flat = lambda ref: ref[...].reshape(-1, ref.shape[-1])
    p1, p2 = up_to(C1 // n, 16), up_to(C2 // n, 16)

    def chunked():
        pick = spread(C1, n)
        hidden_c[...] = dot(flat(hidden_s), pick).astype(bf16)
        pooled_c[...] = dot(flat(pooled_s), pick).astype(bf16)
        narrow_c[...] = dot(flat(narrow_s), spread(C2, n)).astype(bf16)

    @pl.when(jnp.logical_not(last))
    def _():
        for m in range(M):
            full_state(m)
        chunked()

    lax.fori_loop(0, M, backward, 0)

    @pl.when(jnp.logical_not(first))
    def _():
        lax.fori_loop(0, M, stem_out, 0)

    @pl.when(last)
    def _():
        chunked()

    partner = {"dp": dp + 1 - 2 * par}

    def a_copies(q):
        return (
            remote(acc_a.at[q, 1 - par], got_a.at[q], a_ss.at[q, 0], a_rs.at[q, 0], partner),
            remote(acc_d.at[q, 1 - par], got_d.at[q], a_ss.at[q, 1], a_rs.at[q, 1], partner),
        )

    k_copy = remote(gk, got_k, a_ss.at[Q, 0], a_rs.at[Q, 0], partner)
    k_copy.start()
    g_down = dot_outer(pooled_c[...], flat(lift_s))
    acc_d[...] = g_down.reshape(Q, 2, T, p1, C2)
    for q in range(Q):
        a_copies(q)[1].start()
    g_mix = dot_outer(hidden_c[...], flat(total_s))
    acc_a[:, :, :, p2:] = g_mix.reshape(Q, 2, T, p1, C1)
    g_up = dot_outer(narrow_c[...], flat(gnar_s))
    acc_a[:, :, :, 0:p2] = g_up.reshape(Q, 2, T, p2, C1)
    for q in range(Q):
        a_copies(q)[0].start()
    k_copy.wait_recv()
    k_copy.wait_send()
    gk[...] += got_k[...]

    def r_copies(q, h, sq, sh):
        target = {"dp": 2 * q + par, "strip": h}
        pairs = (
            (acc_a.at[q, par, h], far_a.at[sq, sh]),
            (acc_d.at[q, par, h], far_d.at[sq, sh]),
            (gk, far_k.at[sq, sh]),
        )
        return [
            remote(src, dst, r_ss.at[q, h, i], r_rs.at[sq, sh, i], target)
            for i, (src, dst) in enumerate(pairs)
        ]

    for q in range(Q):
        for copy in a_copies(q):
            copy.wait_recv()
        for h in range(T):
            acc_a[q, par, h] += got_a[q, h]
            acc_d[q, par, h] += got_d[q, h]
            other = (mine != q) | (strip != h)

            @pl.when(other)
            def _():
                for copy in r_copies(q, h, mine, strip):
                    copy.start()

            @pl.when(jnp.logical_not(other))
            def _():
                far_a[q, h] = acc_a[q, par, h]
                far_d[q, h] = acc_d[q, par, h]
                far_k[q, h] = gk[...]

    for k in range(S):
        for h in range(T):

            @pl.when((col != k) | (strip != h))
            def _():
                for m in range(M):
                    g_copy(k, h, m, k, h).wait_recv()

    for h in range(T):
        total = gs_recv[0, h]
        for k in range(1, S):
            total = total + gs_recv[k, h]
        o_stem[h * M : (h + 1) * M] = total

    for q in range(Q):
        for h in range(T):

            @pl.when((mine != q) | (strip != h))
            def _():
                for copy in r_copies(q, h, q, h):
                    copy.wait_recv()

    sum_a = sum_d = sum_k = 0.0
    for q in range(Q):
        for h in range(T):
            sum_a = sum_a + far_a[q, h]
            sum_d = sum_d + far_d[q, h]
            sum_k = sum_k + far_k[q, h]
    o_up[...] = sum_a[0 : C2 // n]
    o_mix[...] = sum_a[p2 : p2 + C1 // n]
    o_down[...] = sum_d[0 : C1 // n]
    w = C1 // n
    share = sum_k[0:9, 0:w]
    for k in range(1, n):
        share = jnp.where(dp * T + strip == k, sum_k[0:9, k * w : (k + 1) * w], share)
    o_taps[...] = share

    for m in range(M):
        for h in range(T):

            @pl.when(strip != h)
            def _():
                stem_copy(h, m, strip).wait_send()
                lab_copy(h, m, strip).wait_send()

                @pl.when(jnp.logical_not(last))
                def _():
                    lab_copy(h, m, h).wait_recv()

        for i in range(3):

            @pl.when(jnp.logical_not(last))
            def _():
                f_copy(i, m).wait_send()

            @pl.when(jnp.logical_not(first))
            def _():
                b_copy(i, m).wait_send()

    for k in range(S):
        for h in range(T):

            @pl.when((col != k) | (strip != h))
            def _():
                for m in range(M):
                    g_copy(k, h, m, col, strip).wait_send()

    for q in range(Q):
        for copy in a_copies(q):
            copy.wait_send()
        for h in range(T):

            @pl.when((mine != q) | (strip != h))
            def _():
                for copy in r_copies(q, h, mine, strip):
                    copy.wait_send()


def finish(*refs):
    for source, target in zip(refs[:4], refs[5:9]):
        target[...] = source[...].reshape(target.shape)
    refs[9][...] = refs[4][...]


def shards(stem, labels, up, mix, down, taps, gain1, gain2, lat1, lat2, cls):
    B, rl, W, C1 = stem.shape
    C2 = up.shape[1]
    S, D, T = lax.axis_size("col"), lax.axis_size("dp"), lax.axis_size("strip")
    M = B // T
    RW = rl * W
    pix = T * RW
    small = pix // 4
    wc = W // S
    n = D * T
    Q = D // 2
    p1, p2 = up_to(C1 // n, 16), up_to(C2 // n, 16)
    npix = float(B * D * rl * T * W)
    V = pltpu.VMEM
    dma = pltpu.SemaphoreType.DMA
    vspec = pl.BlockSpec(memory_space=pltpu.VMEM)
    outs = pl.pallas_call(
        functools.partial(kernel, S, D, T, M, rl, W, npix),
        out_shape=(
            jax.ShapeDtypeStruct((C2 // n, C1), f32),
            jax.ShapeDtypeStruct((C1 // n, C1), f32),
            jax.ShapeDtypeStruct((C1 // n, C2), f32),
            jax.ShapeDtypeStruct((9, C1 // n), f32),
            jax.ShapeDtypeStruct((B, rl, wc, C1), f32),
        ),
        in_specs=[vspec] * 11,
        out_specs=(vspec,) * 5,
        scratch_shapes=[
            V((T, M, RW, C1), f32),
            V((M, T, RW, C1), f32),
            V((M, T, rl, W), jnp.int32),
            V((M, pix, C1), f32),
            V((M, small, C2), f32),
            V((M, pix, C1), f32),
            V((M, small, C2), f32),
            V((M, pix, C1), f32),
            V((M, small, C2), f32),
            V((M, pix, C1), f32),
            V((M, small, C2), f32),
            V((M, small, C1), f32),
            V((M, small, C1), f32),
            V((M, small, C1), f32),
            V((M, small, C1), f32),
            V((M, pix, C1), f32),
            V((M * pix, n * p1), bf16),
            V((M * small, n * p1), bf16),
            V((M * small, n * p2), bf16),
            V((pix + 16, C1), f32),
            V((M, pix, C1), f32),
            V((M, pix, C1), f32),
            V((M, pix, C1), bf16),
            V((M, small, C2), bf16),
            V((M, small, C1), bf16),
            V((M, small, C2), f32),
            V((M, pix, C1), bf16),
            V((M, small, C2), bf16),
            V((M, small, C1), bf16),
            V((pix, small), bf16),
            V((small, pix), bf16),
            V((S, T, M, rl, wc, C1), f32),
            V((S, T, M, rl, wc, C1), f32),
            V((Q, 2, T, p1 + p2, C1), f32),
            V((Q, 2, T, p1, C2), f32),
            V((16, C1), f32),
            V((Q, T, p1 + p2, C1), f32),
            V((Q, T, p1, C2), f32),
            V((16, C1), f32),
            V((Q, T, p1 + p2, C1), f32),
            V((Q, T, p1, C2), f32),
            V((Q, T, 16, C1), f32),
            dma((T, M)),
            dma((T, M)),
            dma((T, M)),
            dma((T, M)),
            dma((3, M)),
            dma((3, M)),
            dma((3, M)),
            dma((3, M)),
            dma((S, T, M)),
            dma((S, T, M)),
            dma((Q + 1, 2)),
            dma((Q + 1, 2)),
            dma((Q, T, 3)),
            dma((Q, T, 3)),
        ],
        compiler_params=pltpu.CompilerParams(
            collective_id=0, has_side_effects=True, vmem_limit_bytes=60000 * 1024
        ),
        name="columns",
    )(
        stem.reshape(B, RW, C1), labels, up[0], mix[0], down[0], taps[0], gain1, gain2,
        lat1, lat2, cls.T,
    )
    tall = lambda a: jax.ShapeDtypeStruct((a.shape[0], 1, a.shape[1]), f32)
    done = pl.pallas_call(
        finish,
        out_shape=tuple(tall(a) for a in outs[:4])
        + (jax.ShapeDtypeStruct(outs[4].shape, f32),),
        in_specs=[vspec] * 5,
        out_specs=(vspec,) * 5,
        name="finish",
    )(*outs)
    return tuple(jnp.transpose(a, (1, 0, 2)) for a in done[:4]) + (done[4],)


def solution(mesh):
    placed = (
        P("dp", "strip", None, None),
        P("dp", "strip", None),
        P("col", None, None),
        P("col", None, None),
        P("col", None, None),
        P("col", None, None),
        P("col", None),
        P("col", None),
        P(),
        P(),
        P(),
    )
    return jax.shard_map(
        shards,
        mesh=mesh,
        in_specs=placed,
        out_specs=(
            P("col", ("dp", "strip"), None),
            P("col", ("dp", "strip"), None),
            P("col", ("dp", "strip"), None),
            P("col", None, ("dp", "strip")),
            P("dp", "strip", "col", None),
        ),
        check_vma=False,
    )
```

```python
import functools

import jax
import jax.numpy as jnp
from jax import lax
from jax.experimental import pallas as pl
from jax.experimental.pallas import tpu as pltpu
from jax.sharding import PartitionSpec as P

loss_scale = 64.0
root_coef = 0.7978845608028654
cube_coef = 0.044715
f32 = jnp.float32
bf16 = jnp.bfloat16
MESH = pl.DeviceIdType.MESH


def gelu_pair(values):
    square = values * values
    tangent = jnp.tanh(root_coef * (values + cube_coef * values * square))
    half = 0.5 * (1.0 + tangent)
    slope = half + 0.5 * values * (1.0 - tangent * tangent) * root_coef * (
        1.0 + 3.0 * cube_coef * square
    )
    return values * half, slope


def dot(left, right):
    return jnp.dot(left, right, preferred_element_type=f32)


def dot_back(left, right):
    return lax.dot_general(left, right, (((1,), (1,)), ((), ())), preferred_element_type=f32)


def dot_outer(left, right):
    return lax.dot_general(left, right, (((0,), (0,)), ((), ())), preferred_element_type=f32)


def up_to(count, multiple):
    return -(-count // multiple) * multiple


def spread(count, parts):
    run = count // parts
    padded = up_to(run, 16)
    source = lax.broadcasted_iota(jnp.int32, (count, 1), 0)
    target = source
    for part in range(1, parts):
        target = target + jnp.where(source >= part * run, padded - run, 0)
    spot = lax.broadcasted_iota(jnp.int32, (count, parts * padded), 1)
    return (spot == target).astype(f32).astype(bf16)


def pool_matrix(rows, width, axis_fine):
    fine, coarse = rows * width, rows * width // 4
    shape = (fine, coarse) if axis_fine == 0 else (coarse, fine)
    f = lax.broadcasted_iota(jnp.int32, shape, axis_fine)
    c = lax.broadcasted_iota(jnp.int32, shape, 1 - axis_fine)
    hit = jnp.zeros(shape, jnp.bool_)
    half = width // 2
    for row in range(rows // 2):
        rest = f - row * 2 * width
        inside = (rest >= 0) & (rest < 2 * width)
        rest = jnp.where(rest >= width, rest - width, rest)
        pos = 2 * (c - row * half)
        hit = hit | (inside & ((rest == pos) | (rest == pos + 1)))
    return hit.astype(f32).astype(bf16)


def kernel(
    S, D, T, M, rl, W, npix,
    stem, labels, up, mix, down, taps, gain1, gain2, lat1, lat2, cls,
    o_up, o_mix, o_down, o_taps, o_stem,
    stem_send, stem_full, lab_full, in1, in2, out1, out2, cin1, cin2, cout1, cout2,
    inp, outp, cinp, coutp, branch_s, hidden_c, pooled_c, narrow_c,
    pad, mixture_s, slope1_s, hidden_s, narrow_s, pooled_s, slope2_s, total_s, lift_s, gnar_s,
    spread_u, spread_p, gs_send, gs_recv, acc_a, acc_d, gk, got_a, got_d, got_k,
    far_a, far_d, far_k,
    stem_ss, stem_rs, lab_ss, lab_rs, f_ss, f_rs, b_ss, b_rs, g_ss, g_rs,
    a_ss, a_rs, r_ss, r_rs, ff_ss, ff_rs, bb_ss, bb_rs,
):
    col, dp, strip = lax.axis_index("col"), lax.axis_index("dp"), lax.axis_index("strip")
    first, last = col == 0, col == S - 1
    C1, C2 = up.shape[1], up.shape[0]
    RW = rl * W
    pix = T * RW
    rows = T * rl
    wc = W // S
    par = lax.rem(dp, 2)
    mine = dp // 2
    Q = D // 2

    def remote(src, dst, ss, rs, target):
        return pltpu.make_async_remote_copy(
            src_ref=src, dst_ref=dst, send_sem=ss, recv_sem=rs,
            device_id=target, device_id_type=MESH,
        )

    gate = pltpu.get_barrier_semaphore()
    for h in range(T):
        for k in range(S):

            @pl.when((col != k) | (strip != h))
            def _():
                pl.semaphore_signal(
                    gate, inc=1, device_id={"col": k, "strip": h}, device_id_type=MESH
                )

        for d in range(D):

            @pl.when(dp != d)
            def _():
                pl.semaphore_signal(
                    gate, inc=1, device_id={"dp": d, "strip": h}, device_id_type=MESH
                )

    for m in range(M):
        for h in range(T):
            stem_send[h, m] = stem[h * M + m].astype(f32)

    @pl.when(first)
    def _():
        in1[...] = jnp.zeros_like(in1)
        in2[...] = jnp.zeros_like(in2)
        inp[...] = jnp.zeros_like(inp)

    @pl.when(last)
    def _():
        cinp[...] = jnp.zeros_like(cinp)

    pad[...] = jnp.zeros_like(pad)
    gk[...] = jnp.zeros_like(gk)
    spread_u[...] = pool_matrix(rows, W, 0)
    spread_p[...] = pool_matrix(rows, W, 1)
    pl.semaphore_wait(gate, S * T - 1 + (D - 1) * T)

    def stem_copy(h, m, slot):
        return remote(
            stem_send.at[h, m], stem_full.at[m, slot], stem_ss.at[h, m], stem_rs.at[slot, m],
            {"strip": h},
        )

    def lab_copy(h, m, slot):
        return remote(
            labels.at[h * M + m], lab_full.at[m, slot], lab_ss.at[h, m], lab_rs.at[slot, m],
            {"strip": h},
        )

    for m in range(M):
        for h in range(T):
            @pl.when(strip != h)
            def _():
                stem_copy(h, m, strip).start()
    for m in range(M):
        for h in range(T):

            @pl.when(strip != h)
            def _():
                lab_copy(h, m, strip).start()

            @pl.when(strip == h)
            def _():
                stem_full[m, h] = stem[h * M + m].astype(f32)
                lab_full[m, h] = labels[h * M + m]

    kern = taps[0:9].astype(f32)
    g1 = gain1[...]
    g2 = gain2[...]
    place = lax.rem(lax.broadcasted_iota(jnp.int32, (pix, 1), 0), W)
    not_low = place != 0
    not_high = place != W - 1

    def widen(values):
        return dot(spread_u[...], values).astype(bf16)

    def pool(values):
        high = values.astype(bf16)
        low = (values - high.astype(f32)).astype(bf16)
        return dot(spread_p[...], high) + dot(spread_p[...], low)

    def sides(values):
        pad[8 : 8 + pix] = values
        before = jnp.where(not_low, pad[7 : 7 + pix], 0.0)
        after = jnp.where(not_high, pad[9 : 9 + pix], 0.0)
        return before, values, after

    def rows_moved(values, step):
        if step == 0:
            return values
        blank = jnp.zeros((W, values.shape[1]), f32)
        if step > 0:
            return jnp.concatenate([values[W:], blank], axis=0)
        return jnp.concatenate([blank, values[:-W]], axis=0)

    def depthwise(values, sign):
        trio = sides(values)
        total = None
        for i in (-1, 0, 1):
            line = None
            for j in (-1, 0, 1):
                t = 3 * (i + 1) + (j + 1)
                term = kern[t : t + 1] * trio[1 + sign * j]
                line = term if line is None else line + term
            line = rows_moved(line, sign * i)
            total = line if total is None else total + line
        return total

    def f_copy(n, m):
        src, dst = (None, (out2, in2), (outp, inp))[n]
        return remote(src.at[m], dst.at[m], f_ss.at[n, m], f_rs.at[n, m], {"col": col + 1})

    def b_copy(n, m):
        src, dst = (None, (cout2, cin2), (coutp, cinp))[n]
        return remote(src.at[m], dst.at[m], b_ss.at[n, m], b_rs.at[n, m], {"col": col - 1})

    def f_row(m, r):
        part = pl.ds(r * W, W)
        return remote(
            out1.at[m, part], in1.at[m, part], ff_ss.at[m, r], ff_rs.at[m, r], {"col": col + 1}
        )

    def b_row(m, r):
        part = pl.ds(r * W, W)
        return remote(
            cout1.at[m, part], cin1.at[m, part], bb_ss.at[m, r], bb_rs.at[m, r],
            {"col": col - 1},
        )

    def forward(m, carry):
        for h in range(T):

            @pl.when(strip != h)
            def _():
                stem_copy(h, m, h).wait_recv()

        @pl.when(jnp.logical_not(first))
        def _():
            f_copy(1, m).wait_recv()

        narrow = in2[m].astype(bf16)
        narrow_s[m] = narrow
        mixture = stem_full[m].reshape(pix, C1) + dot(widen(narrow), up[...])
        mixture_s[m] = mixture
        active, slope = gelu_pair(depthwise(mixture, 1))
        slope1_s[m] = slope
        hidden = active.astype(bf16)
        hidden_s[m] = hidden
        branch = dot(hidden, mix[...])
        branch_s[m] = branch
        pool_branch = pool(branch)

        @pl.when(jnp.logical_not(first))
        def _():
            f_copy(2, m).wait_recv()

        low1 = g1 * inp[m] + pool_branch
        outp[m] = low1
        pooled = (low1 * 0.25).astype(bf16)
        pooled_s[m] = pooled
        lifted, slope2 = gelu_pair(dot(pooled, down[...]))
        slope2_s[m] = slope2
        out2[m] = g2 * in2[m] + lifted

        @pl.when(jnp.logical_not(last))
        def _():
            f_copy(1, m).start()
            f_copy(2, m).start()

        return carry

    lax.fori_loop(0, M, forward, 0)

    def full_state(m):
        for r in range(rows):

            @pl.when(jnp.logical_not(first))
            def _():
                f_row(m, r).wait_recv()

            part = pl.ds(r * W, W)
            out1[m, part] = g1 * in1[m, part] + branch_s[m, part]

            @pl.when(jnp.logical_not(last))
            def _():
                f_row(m, r).start()

    def g_copy(k, h, m, sk, sh):
        return remote(
            gs_send.at[k, h, m], gs_recv.at[sk, sh, m], g_ss.at[k, h, m], g_rs.at[sk, sh, m],
            {"col": k, "strip": h},
        )

    def stem_out(m, carry):
        for k in range(S):
            for h in range(T):
                other = (col != k) | (strip != h)

                @pl.when(other)
                def _():
                    g_copy(k, h, m, col, strip).start()

                @pl.when(jnp.logical_not(other))
                def _():
                    gs_recv[k, h, m] = gs_send[k, h, m]

        return carry

    def backward(m, carry):
        @pl.when(last)
        def _():
            full_state(m)
            for h in range(T):

                @pl.when(strip != h)
                def _():
                    lab_copy(h, m, h).wait_recv()

            lateral = dot(out1[m].astype(bf16), lat1[...]) + dot(
                widen(out2[m].astype(bf16)), lat2[...]
            )
            active, slope = gelu_pair(lateral)
            logits = dot_back(active.astype(bf16), cls[...])
            shifted = jnp.exp(logits - jnp.max(logits, axis=-1, keepdims=True))
            probs = shifted / jnp.sum(shifted, axis=-1, keepdims=True)
            eye = lax.broadcasted_iota(jnp.int32, (W, W), 0) == lax.broadcasted_iota(
                jnp.int32, (W, W), 1
            )
            lines = []
            for h in range(T):
                block = lab_full[m, h].astype(f32)
                for r in range(rl):
                    turned = jnp.where(eye, block[r : r + 1], 0.0)
                    lines.append(jnp.sum(turned, axis=1, keepdims=True))
            label = jnp.concatenate(lines, axis=0).astype(jnp.int32)
            onehot = (lax.broadcasted_iota(jnp.int32, logits.shape, 1) == label).astype(f32)
            grad_logits = (probs - onehot) * (loss_scale / npix)
            grad_lat = dot(grad_logits.astype(bf16), cls[...]) * slope
            cin1[m] = dot_back(grad_lat.astype(bf16), lat1[...])
            cin2[m] = dot_back(pool(grad_lat).astype(bf16), lat2[...])

        for r in range(rows):

            @pl.when(jnp.logical_not(last))
            def _():
                b_row(m, r).wait_recv()

            @pl.when(jnp.logical_not(first))
            def _():
                part = pl.ds(r * W, W)
                cout1[m, part] = g1 * cin1[m, part]
                b_row(m, r).start()

        @pl.when(jnp.logical_not(last))
        def _():
            b_copy(1, m).wait_recv()

        cot2 = cin2[m]
        lift = (cot2 * slope2_s[m]).astype(bf16)
        lift_s[m] = lift
        rise = dot_back(lift, down[...]) * 0.25

        @pl.when(jnp.logical_not(last))
        def _():
            b_copy(2, m).wait_recv()

        rise = cinp[m] + rise

        @pl.when(jnp.logical_not(first))
        def _():
            coutp[m] = g1 * rise
            b_copy(2, m).start()

        high = rise.astype(bf16)
        low = (rise - high.astype(f32)).astype(bf16)
        total = cin1[m] + (dot(spread_u[...], high) + dot(spread_u[...], low))
        total_narrow = total.astype(bf16)
        total_s[m] = total_narrow
        grad_depth = dot_back(total_narrow, mix[...]) * slope1_s[m]
        grad_mixture = depthwise(grad_depth, -1)
        grad_narrow = pool(grad_mixture).astype(bf16)
        gnar_s[m] = grad_narrow
        cout2[m] = g2 * cot2 + dot_back(grad_narrow, up[...])

        @pl.when(jnp.logical_not(first))
        def _():
            b_copy(1, m).start()

        cube = grad_mixture.reshape(rows, W, C1)
        for k in range(S):
            for h in range(T):
                gs_send[k, h, m] = cube[h * rl : (h + 1) * rl, k * wc : (k + 1) * wc]
        @pl.when(first)
        def _():
            stem_out(m, 0)

        trio = sides(mixture_s[m])
        for i in (-1, 0, 1):
            for j in (-1, 0, 1):
                t = 3 * (i + 1) + (j + 1)
                window = rows_moved(trio[1 + j], i)
                gk[t : t + 1] += jnp.sum(window * grad_depth, axis=0, keepdims=True)
        return carry

    n = D * T
    flat = lambda ref: ref[...].reshape(-1, ref.shape[-1])
    p1, p2 = up_to(C1 // n, 16), up_to(C2 // n, 16)

    def chunked():
        pick = spread(C1, n)
        hidden_c[...] = dot(flat(hidden_s), pick).astype(bf16)
        pooled_c[...] = dot(flat(pooled_s), pick).astype(bf16)
        narrow_c[...] = dot(flat(narrow_s), spread(C2, n)).astype(bf16)

    @pl.when(jnp.logical_not(last))
    def _():
        for m in range(M):
            full_state(m)
        chunked()

    lax.fori_loop(0, M, backward, 0)

    @pl.when(jnp.logical_not(first))
    def _():
        lax.fori_loop(0, M, stem_out, 0)

    @pl.when(last)
    def _():
        chunked()

    partner = {"dp": dp + 1 - 2 * par}

    def a_copies(q):
        return (
            remote(acc_a.at[q, 1 - par], got_a.at[q], a_ss.at[q, 0], a_rs.at[q, 0], partner),
            remote(acc_d.at[q, 1 - par], got_d.at[q], a_ss.at[q, 1], a_rs.at[q, 1], partner),
        )

    k_copy = remote(gk, got_k, a_ss.at[Q, 0], a_rs.at[Q, 0], partner)
    k_copy.start()
    g_down = dot_outer(pooled_c[...], flat(lift_s))
    acc_d[...] = g_down.reshape(Q, 2, T, p1, C2)
    for q in range(Q):
        a_copies(q)[1].start()
    g_mix = dot_outer(hidden_c[...], flat(total_s))
    acc_a[:, :, :, p2:] = g_mix.reshape(Q, 2, T, p1, C1)
    g_up = dot_outer(narrow_c[...], flat(gnar_s))
    acc_a[:, :, :, 0:p2] = g_up.reshape(Q, 2, T, p2, C1)
    for q in range(Q):
        a_copies(q)[0].start()
    k_copy.wait_recv()
    k_copy.wait_send()
    gk[...] += got_k[...]

    def r_copies(q, h, sq, sh):
        target = {"dp": 2 * q + par, "strip": h}
        pairs = (
            (acc_a.at[q, par, h], far_a.at[sq, sh]),
            (acc_d.at[q, par, h], far_d.at[sq, sh]),
            (gk, far_k.at[sq, sh]),
        )
        return [
            remote(src, dst, r_ss.at[q, h, i], r_rs.at[sq, sh, i], target)
            for i, (src, dst) in enumerate(pairs)
        ]

    def pass_on(i, q, own, total):
        for h in range(T):
            other = (mine != q) | (strip != h)

            @pl.when(other)
            def _():
                r_copies(q, h, mine, strip)[i].start()

            @pl.when(jnp.logical_not(other))
            def _():
                own[q, h] = total(h)[...]

    for q in range(Q):
        pass_on(2, q, far_k, lambda h: gk)
    for i, acc, got, far in ((1, acc_d, got_d, far_d), (0, acc_a, got_a, far_a)):
        for q in range(Q):
            a_copies(q)[i].wait_recv()
            for h in range(T):
                acc[q, par, h] += got[q, h]
            pass_on(i, q, far, lambda h: acc.at[q, par, h])

    for k in range(S):
        for h in range(T):

            @pl.when((col != k) | (strip != h))
            def _():
                for m in range(M):
                    g_copy(k, h, m, k, h).wait_recv()

    for h in range(T):
        total = gs_recv[0, h]
        for k in range(1, S):
            total = total + gs_recv[k, h]
        o_stem[h * M : (h + 1) * M] = total

    for q in range(Q):
        for h in range(T):

            @pl.when((mine != q) | (strip != h))
            def _():
                for copy in r_copies(q, h, q, h):
                    copy.wait_recv()

    sum_a = sum_d = sum_k = 0.0
    for q in range(Q):
        for h in range(T):
            sum_a = sum_a + far_a[q, h]
            sum_d = sum_d + far_d[q, h]
            sum_k = sum_k + far_k[q, h]
    o_up[...] = sum_a[0 : C2 // n]
    o_mix[...] = sum_a[p2 : p2 + C1 // n]
    o_down[...] = sum_d[0 : C1 // n]
    w = C1 // n
    share = sum_k[0:9, 0:w]
    for k in range(1, n):
        share = jnp.where(dp * T + strip == k, sum_k[0:9, k * w : (k + 1) * w], share)
    o_taps[...] = share

    for m in range(M):
        for h in range(T):

            @pl.when(strip != h)
            def _():
                stem_copy(h, m, strip).wait_send()
                lab_copy(h, m, strip).wait_send()

                @pl.when(jnp.logical_not(last))
                def _():
                    lab_copy(h, m, h).wait_recv()

        @pl.when(jnp.logical_not(last))
        def _():
            f_copy(1, m).wait_send()
            f_copy(2, m).wait_send()
            for r in range(rows):
                f_row(m, r).wait_send()

        @pl.when(jnp.logical_not(first))
        def _():
            b_copy(1, m).wait_send()
            b_copy(2, m).wait_send()
            for r in range(rows):
                b_row(m, r).wait_send()

    for k in range(S):
        for h in range(T):

            @pl.when((col != k) | (strip != h))
            def _():
                for m in range(M):
                    g_copy(k, h, m, col, strip).wait_send()

    for q in range(Q):
        for copy in a_copies(q):
            copy.wait_send()
        for h in range(T):

            @pl.when((mine != q) | (strip != h))
            def _():
                for copy in r_copies(q, h, mine, strip):
                    copy.wait_send()


def finish(*refs):
    for source, target in zip(refs[:4], refs[5:9]):
        target[...] = source[...].reshape(target.shape)
    refs[9][...] = refs[4][...]


def shards(stem, labels, up, mix, down, taps, gain1, gain2, lat1, lat2, cls):
    B, rl, W, C1 = stem.shape
    C2 = up.shape[1]
    S, D, T = lax.axis_size("col"), lax.axis_size("dp"), lax.axis_size("strip")
    M = B // T
    RW = rl * W
    pix = T * RW
    small = pix // 4
    wc = W // S
    n = D * T
    Q = D // 2
    p1, p2 = up_to(C1 // n, 16), up_to(C2 // n, 16)
    npix = float(B * D * rl * T * W)
    V = pltpu.VMEM
    dma = pltpu.SemaphoreType.DMA
    vspec = pl.BlockSpec(memory_space=pltpu.VMEM)
    outs = pl.pallas_call(
        functools.partial(kernel, S, D, T, M, rl, W, npix),
        out_shape=(
            jax.ShapeDtypeStruct((C2 // n, C1), f32),
            jax.ShapeDtypeStruct((C1 // n, C1), f32),
            jax.ShapeDtypeStruct((C1 // n, C2), f32),
            jax.ShapeDtypeStruct((9, C1 // n), f32),
            jax.ShapeDtypeStruct((B, rl, wc, C1), f32),
        ),
        in_specs=[vspec] * 11,
        out_specs=(vspec,) * 5,
        scratch_shapes=[
            V((T, M, RW, C1), f32),
            V((M, T, RW, C1), f32),
            V((M, T, rl, W), jnp.int32),
            V((M, pix, C1), f32),
            V((M, small, C2), f32),
            V((M, pix, C1), f32),
            V((M, small, C2), f32),
            V((M, pix, C1), f32),
            V((M, small, C2), f32),
            V((M, pix, C1), f32),
            V((M, small, C2), f32),
            V((M, small, C1), f32),
            V((M, small, C1), f32),
            V((M, small, C1), f32),
            V((M, small, C1), f32),
            V((M, pix, C1), f32),
            V((M * pix, n * p1), bf16),
            V((M * small, n * p1), bf16),
            V((M * small, n * p2), bf16),
            V((pix + 16, C1), f32),
            V((M, pix, C1), f32),
            V((M, pix, C1), f32),
            V((M, pix, C1), bf16),
            V((M, small, C2), bf16),
            V((M, small, C1), bf16),
            V((M, small, C2), f32),
            V((M, pix, C1), bf16),
            V((M, small, C2), bf16),
            V((M, small, C1), bf16),
            V((pix, small), bf16),
            V((small, pix), bf16),
            V((S, T, M, rl, wc, C1), f32),
            V((S, T, M, rl, wc, C1), f32),
            V((Q, 2, T, p1 + p2, C1), f32),
            V((Q, 2, T, p1, C2), f32),
            V((16, C1), f32),
            V((Q, T, p1 + p2, C1), f32),
            V((Q, T, p1, C2), f32),
            V((16, C1), f32),
            V((Q, T, p1 + p2, C1), f32),
            V((Q, T, p1, C2), f32),
            V((Q, T, 16, C1), f32),
            dma((T, M)),
            dma((T, M)),
            dma((T, M)),
            dma((T, M)),
            dma((3, M)),
            dma((3, M)),
            dma((3, M)),
            dma((3, M)),
            dma((S, T, M)),
            dma((S, T, M)),
            dma((Q + 1, 2)),
            dma((Q + 1, 2)),
            dma((Q, T, 3)),
            dma((Q, T, 3)),
            dma((M, T * rl)),
            dma((M, T * rl)),
            dma((M, T * rl)),
            dma((M, T * rl)),
        ],
        compiler_params=pltpu.CompilerParams(
            collective_id=0, has_side_effects=True, vmem_limit_bytes=60000 * 1024
        ),
        name="columns",
    )(
        stem.reshape(B, RW, C1), labels, up[0], mix[0], down[0], taps[0], gain1, gain2,
        lat1, lat2, cls.T,
    )
    tall = lambda a: jax.ShapeDtypeStruct((a.shape[0], 1, a.shape[1]), f32)
    done = pl.pallas_call(
        finish,
        out_shape=tuple(tall(a) for a in outs[:4])
        + (jax.ShapeDtypeStruct(outs[4].shape, f32),),
        in_specs=[vspec] * 5,
        out_specs=(vspec,) * 5,
        name="finish",
    )(*outs)
    return tuple(jnp.transpose(a, (1, 0, 2)) for a in done[:4]) + (done[4],)


def solution(mesh):
    placed = (
        P("dp", "strip", None, None),
        P("dp", "strip", None),
        P("col", None, None),
        P("col", None, None),
        P("col", None, None),
        P("col", None, None),
        P("col", None),
        P("col", None),
        P(),
        P(),
        P(),
    )
    return jax.shard_map(
        shards,
        mesh=mesh,
        in_specs=placed,
        out_specs=(
            P("col", ("dp", "strip"), None),
            P("col", ("dp", "strip"), None),
            P("col", ("dp", "strip"), None),
            P("col", None, ("dp", "strip")),
            P("dp", "strip", "col", None),
        ),
        check_vma=False,
    )
```

```python
import functools

import jax
import jax.numpy as jnp
from jax import lax
from jax.experimental import pallas as pl
from jax.experimental.pallas import tpu as pltpu
from jax.sharding import PartitionSpec as P

loss_scale = 64.0
root_coef = 0.7978845608028654
cube_coef = 0.044715
f32 = jnp.float32
bf16 = jnp.bfloat16
MESH = pl.DeviceIdType.MESH


def gelu_pair(values):
    square = values * values
    tangent = jnp.tanh(root_coef * (values + cube_coef * values * square))
    half = 0.5 * (1.0 + tangent)
    slope = half + 0.5 * values * (1.0 - tangent * tangent) * root_coef * (
        1.0 + 3.0 * cube_coef * square
    )
    return values * half, slope


def dot(left, right):
    return jnp.dot(left, right, preferred_element_type=f32)


def dot_back(left, right):
    return lax.dot_general(left, right, (((1,), (1,)), ((), ())), preferred_element_type=f32)


def dot_outer(left, right):
    return lax.dot_general(left, right, (((0,), (0,)), ((), ())), preferred_element_type=f32)


def up_to(count, multiple):
    return -(-count // multiple) * multiple


def spread(count, parts):
    run = count // parts
    padded = up_to(run, 16)
    source = lax.broadcasted_iota(jnp.int32, (count, 1), 0)
    target = source
    for part in range(1, parts):
        target = target + jnp.where(source >= part * run, padded - run, 0)
    spot = lax.broadcasted_iota(jnp.int32, (count, parts * padded), 1)
    return (spot == target).astype(f32).astype(bf16)


def pool_matrix(rows, width, axis_fine):
    fine, coarse = rows * width, rows * width // 4
    shape = (fine, coarse) if axis_fine == 0 else (coarse, fine)
    f = lax.broadcasted_iota(jnp.int32, shape, axis_fine)
    c = lax.broadcasted_iota(jnp.int32, shape, 1 - axis_fine)
    hit = jnp.zeros(shape, jnp.bool_)
    half = width // 2
    for row in range(rows // 2):
        rest = f - row * 2 * width
        inside = (rest >= 0) & (rest < 2 * width)
        rest = jnp.where(rest >= width, rest - width, rest)
        pos = 2 * (c - row * half)
        hit = hit | (inside & ((rest == pos) | (rest == pos + 1)))
    return hit.astype(f32).astype(bf16)


def kernel(
    S, D, T, M, rl, W, npix,
    stem, labels, up, mix, down, taps, gain1, gain2, lat1, lat2, cls,
    o_up, o_mix, o_down, o_taps, o_stem,
    stem_send, stem_full, lab_full, in1, in2, out1, out2, cin1, cin2, cout1, cout2,
    inp, outp, cinp, coutp, branch_s, hidden_c, pooled_c, narrow_c,
    pad, mixture_s, slope1_s, hidden_s, narrow_s, pooled_s, slope2_s, total_s, lift_s, gnar_s,
    spread_u, spread_p, gs_send, gs_recv, acc_a, acc_d, gk, got_a, got_d, got_k,
    far_a, far_d, far_k,
    stem_ss, stem_rs, lab_ss, lab_rs, f_ss, f_rs, b_ss, b_rs, g_ss, g_rs,
    a_ss, a_rs, r_ss, r_rs, ff_ss, ff_rs, bb_ss, bb_rs,
):
    col, dp, strip = lax.axis_index("col"), lax.axis_index("dp"), lax.axis_index("strip")
    first, last = col == 0, col == S - 1
    C1, C2 = up.shape[1], up.shape[0]
    RW = rl * W
    pix = T * RW
    rows = T * rl
    wc = W // S
    par = lax.rem(dp, 2)
    mine = dp // 2
    Q = D // 2

    def remote(src, dst, ss, rs, target):
        return pltpu.make_async_remote_copy(
            src_ref=src, dst_ref=dst, send_sem=ss, recv_sem=rs,
            device_id=target, device_id_type=MESH,
        )

    gate = pltpu.get_barrier_semaphore()
    for h in range(T):
        for k in range(S):

            @pl.when((col != k) | (strip != h))
            def _():
                pl.semaphore_signal(
                    gate, inc=1, device_id={"col": k, "strip": h}, device_id_type=MESH
                )

        for d in range(D):

            @pl.when(dp != d)
            def _():
                pl.semaphore_signal(
                    gate, inc=1, device_id={"dp": d, "strip": h}, device_id_type=MESH
                )

    for m in range(M):
        for h in range(T):
            stem_send[h, m] = stem[h * M + m].astype(f32)

    @pl.when(first)
    def _():
        in1[...] = jnp.zeros_like(in1)
        in2[...] = jnp.zeros_like(in2)
        inp[...] = jnp.zeros_like(inp)

    @pl.when(last)
    def _():
        cinp[...] = jnp.zeros_like(cinp)

    pad[...] = jnp.zeros_like(pad)
    gk[...] = jnp.zeros_like(gk)
    spread_u[...] = pool_matrix(rows, W, 0)
    spread_p[...] = pool_matrix(rows, W, 1)
    pl.semaphore_wait(gate, S * T - 1 + (D - 1) * T)

    def stem_copy(h, m, slot):
        return remote(
            stem_send.at[h, m], stem_full.at[m, slot], stem_ss.at[h, m], stem_rs.at[slot, m],
            {"strip": h},
        )

    def lab_copy(h, m, slot):
        return remote(
            labels.at[h * M + m], lab_full.at[m, slot], lab_ss.at[h, m], lab_rs.at[slot, m],
            {"strip": h},
        )

    for m in range(M):
        for h in range(T):
            @pl.when(strip != h)
            def _():
                stem_copy(h, m, strip).start()
    for m in range(M):
        for h in range(T):

            @pl.when(strip != h)
            def _():
                lab_copy(h, m, strip).start()

            @pl.when(strip == h)
            def _():
                stem_full[m, h] = stem[h * M + m].astype(f32)
                lab_full[m, h] = labels[h * M + m]

    kern = taps[0:9].astype(f32)
    g1 = gain1[...]
    g2 = gain2[...]
    place = lax.rem(lax.broadcasted_iota(jnp.int32, (pix, 1), 0), W)
    not_low = place != 0
    not_high = place != W - 1

    def widen(values):
        return dot(spread_u[...], values).astype(bf16)

    def pool(values):
        high = values.astype(bf16)
        low = (values - high.astype(f32)).astype(bf16)
        return dot(spread_p[...], high) + dot(spread_p[...], low)

    def sides(values):
        pad[8 : 8 + pix] = values
        before = jnp.where(not_low, pad[7 : 7 + pix], 0.0)
        after = jnp.where(not_high, pad[9 : 9 + pix], 0.0)
        return before, values, after

    def rows_moved(values, step):
        if step == 0:
            return values
        blank = jnp.zeros((W, values.shape[1]), f32)
        if step > 0:
            return jnp.concatenate([values[W:], blank], axis=0)
        return jnp.concatenate([blank, values[:-W]], axis=0)

    def depthwise(values, sign):
        trio = sides(values)
        total = None
        for i in (-1, 0, 1):
            line = None
            for j in (-1, 0, 1):
                t = 3 * (i + 1) + (j + 1)
                term = kern[t : t + 1] * trio[1 + sign * j]
                line = term if line is None else line + term
            line = rows_moved(line, sign * i)
            total = line if total is None else total + line
        return total

    def f_copy(n, m):
        src, dst = (None, (out2, in2), (outp, inp))[n]
        return remote(src.at[m], dst.at[m], f_ss.at[n, m], f_rs.at[n, m], {"col": col + 1})

    def b_copy(n, m):
        src, dst = (None, (cout2, cin2), (coutp, cinp))[n]
        return remote(src.at[m], dst.at[m], b_ss.at[n, m], b_rs.at[n, m], {"col": col - 1})

    def f_row(m, r):
        part = pl.ds(r * W, W)
        return remote(
            out1.at[m, part], in1.at[m, part], ff_ss.at[m, r], ff_rs.at[m, r], {"col": col + 1}
        )

    def b_row(m, r):
        part = pl.ds(r * W, W)
        return remote(
            cout1.at[m, part], cin1.at[m, part], bb_ss.at[m, r], bb_rs.at[m, r],
            {"col": col - 1},
        )

    def forward(m, carry):
        for h in range(T):

            @pl.when(strip != h)
            def _():
                stem_copy(h, m, h).wait_recv()

        @pl.when(jnp.logical_not(first))
        def _():
            f_copy(1, m).wait_recv()

        narrow = in2[m].astype(bf16)
        narrow_s[m] = narrow
        mixture = stem_full[m].reshape(pix, C1) + dot(widen(narrow), up[...])
        mixture_s[m] = mixture
        active, slope = gelu_pair(depthwise(mixture, 1))
        slope1_s[m] = slope
        hidden = active.astype(bf16)
        hidden_s[m] = hidden
        branch = dot(hidden, mix[...])
        branch_s[m] = branch
        pool_branch = pool(branch)

        @pl.when(jnp.logical_not(first))
        def _():
            f_copy(2, m).wait_recv()

        low1 = g1 * inp[m] + pool_branch
        outp[m] = low1
        pooled = (low1 * 0.25).astype(bf16)
        pooled_s[m] = pooled
        lifted, slope2 = gelu_pair(dot(pooled, down[...]))
        slope2_s[m] = slope2
        out2[m] = g2 * in2[m] + lifted

        @pl.when(jnp.logical_not(last))
        def _():
            f_copy(1, m).start()
            f_copy(2, m).start()

        return carry

    lax.fori_loop(0, M, forward, 0)

    def full_state(m):
        for r in range(rows):

            @pl.when(jnp.logical_not(first))
            def _():
                f_row(m, r).wait_recv()

            part = pl.ds(r * W, W)
            out1[m, part] = g1 * in1[m, part] + branch_s[m, part]

            @pl.when(jnp.logical_not(last))
            def _():
                f_row(m, r).start()

    def g_copy(k, h, m, sk, sh):
        return remote(
            gs_send.at[k, h, m], gs_recv.at[sk, sh, m], g_ss.at[k, h, m], g_rs.at[sk, sh, m],
            {"col": k, "strip": h},
        )

    def stem_out(m, carry):
        for k in range(S):
            for h in range(T):
                other = (col != k) | (strip != h)

                @pl.when(other)
                def _():
                    g_copy(k, h, m, col, strip).start()

                @pl.when(jnp.logical_not(other))
                def _():
                    gs_recv[k, h, m] = gs_send[k, h, m]

        return carry

    def backward(m, carry):
        @pl.when(last)
        def _():
            full_state(m)
            for h in range(T):

                @pl.when(strip != h)
                def _():
                    lab_copy(h, m, h).wait_recv()

            lateral = dot(out1[m].astype(bf16), lat1[...]) + dot(
                widen(out2[m].astype(bf16)), lat2[...]
            )
            active, slope = gelu_pair(lateral)
            logits = dot_back(active.astype(bf16), cls[...])
            shifted = jnp.exp(logits - jnp.max(logits, axis=-1, keepdims=True))
            probs = shifted / jnp.sum(shifted, axis=-1, keepdims=True)
            eye = lax.broadcasted_iota(jnp.int32, (W, W), 0) == lax.broadcasted_iota(
                jnp.int32, (W, W), 1
            )
            lines = []
            for h in range(T):
                block = lab_full[m, h].astype(f32)
                for r in range(rl):
                    turned = jnp.where(eye, block[r : r + 1], 0.0)
                    lines.append(jnp.sum(turned, axis=1, keepdims=True))
            label = jnp.concatenate(lines, axis=0).astype(jnp.int32)
            onehot = (lax.broadcasted_iota(jnp.int32, logits.shape, 1) == label).astype(f32)
            grad_logits = (probs - onehot) * (loss_scale / npix)
            grad_lat = dot(grad_logits.astype(bf16), cls[...]) * slope
            cin1[m] = dot_back(grad_lat.astype(bf16), lat1[...])
            cin2[m] = dot_back(pool(grad_lat).astype(bf16), lat2[...])

        for r in range(rows):

            @pl.when(jnp.logical_not(last))
            def _():
                b_row(m, r).wait_recv()

            @pl.when(jnp.logical_not(first))
            def _():
                part = pl.ds(r * W, W)
                cout1[m, part] = g1 * cin1[m, part]
                b_row(m, r).start()

        @pl.when(jnp.logical_not(last))
        def _():
            b_copy(1, m).wait_recv()

        cot2 = cin2[m]
        lift = (cot2 * slope2_s[m]).astype(bf16)
        lift_s[m] = lift
        rise = dot_back(lift, down[...]) * 0.25

        @pl.when(jnp.logical_not(last))
        def _():
            b_copy(2, m).wait_recv()

        rise = cinp[m] + rise

        @pl.when(jnp.logical_not(first))
        def _():
            coutp[m] = g1 * rise
            b_copy(2, m).start()

        high = rise.astype(bf16)
        low = (rise - high.astype(f32)).astype(bf16)
        total = cin1[m] + (dot(spread_u[...], high) + dot(spread_u[...], low))
        total_narrow = total.astype(bf16)
        total_s[m] = total_narrow
        grad_depth = dot_back(total_narrow, mix[...]) * slope1_s[m]
        grad_mixture = depthwise(grad_depth, -1)
        grad_narrow = pool(grad_mixture).astype(bf16)
        gnar_s[m] = grad_narrow
        cout2[m] = g2 * cot2 + dot_back(grad_narrow, up[...])

        @pl.when(jnp.logical_not(first))
        def _():
            b_copy(1, m).start()

        cube = grad_mixture.reshape(rows, W, C1)
        for k in range(S):
            for h in range(T):
                gs_send[k, h, m] = cube[h * rl : (h + 1) * rl, k * wc : (k + 1) * wc]
        @pl.when(first)
        def _():
            stem_out(m, 0)

        trio = sides(mixture_s[m])
        for i in (-1, 0, 1):
            for j in (-1, 0, 1):
                t = 3 * (i + 1) + (j + 1)
                window = rows_moved(trio[1 + j], i)
                gk[t : t + 1] += jnp.sum(window * grad_depth, axis=0, keepdims=True)
        return carry

    n = D * T
    flat = lambda ref: ref[...].reshape(-1, ref.shape[-1])
    p1, p2 = up_to(C1 // n, 16), up_to(C2 // n, 16)

    def chunked():
        pick = spread(C1, n)
        hidden_c[...] = dot(flat(hidden_s), pick).astype(bf16)
        pooled_c[...] = dot(flat(pooled_s), pick).astype(bf16)
        narrow_c[...] = dot(flat(narrow_s), spread(C2, n)).astype(bf16)

    @pl.when(jnp.logical_not(last))
    def _():
        for m in range(M):
            full_state(m)
        chunked()

    lax.fori_loop(0, M, backward, 0)

    @pl.when(last)
    def _():
        chunked()

    partner = {"dp": dp + 1 - 2 * par}

    def a_copies(q):
        return (
            remote(acc_a.at[q, 1 - par], got_a.at[q], a_ss.at[q, 0], a_rs.at[q, 0], partner),
            remote(acc_d.at[q, 1 - par], got_d.at[q], a_ss.at[q, 1], a_rs.at[q, 1], partner),
        )

    k_copy = remote(gk, got_k, a_ss.at[Q, 0], a_rs.at[Q, 0], partner)
    k_copy.start()
    g_down = dot_outer(pooled_c[...], flat(lift_s))
    acc_d[...] = g_down.reshape(Q, 2, T, p1, C2)
    for q in range(Q):
        a_copies(q)[1].start()
    g_mix = dot_outer(hidden_c[...], flat(total_s))
    acc_a[:, :, :, p2:] = g_mix.reshape(Q, 2, T, p1, C1)
    g_up = dot_outer(narrow_c[...], flat(gnar_s))
    acc_a[:, :, :, 0:p2] = g_up.reshape(Q, 2, T, p2, C1)
    for q in range(Q):
        a_copies(q)[0].start()
    k_copy.wait_recv()
    k_copy.wait_send()
    gk[...] += got_k[...]

    def r_copies(q, h, sq, sh):
        target = {"dp": 2 * q + par, "strip": h}
        pairs = (
            (acc_a.at[q, par, h], far_a.at[sq, sh]),
            (acc_d.at[q, par, h], far_d.at[sq, sh]),
            (gk, far_k.at[sq, sh]),
        )
        return [
            remote(src, dst, r_ss.at[q, h, i], r_rs.at[sq, sh, i], target)
            for i, (src, dst) in enumerate(pairs)
        ]

    def pass_on(i, q, own, total):
        for h in range(T):
            other = (mine != q) | (strip != h)

            @pl.when(other)
            def _():
                r_copies(q, h, mine, strip)[i].start()

            @pl.when(jnp.logical_not(other))
            def _():
                own[q, h] = total(h)[...]

    for q in range(Q):
        pass_on(2, q, far_k, lambda h: gk)
    for i, acc, got, far in ((1, acc_d, got_d, far_d), (0, acc_a, got_a, far_a)):
        for q in range(Q):
            a_copies(q)[i].wait_recv()
            for h in range(T):
                acc[q, par, h] += got[q, h]
            pass_on(i, q, far, lambda h: acc.at[q, par, h])

    for q in range(Q):
        for h in range(T):

            @pl.when((mine != q) | (strip != h))
            def _():
                for copy in r_copies(q, h, q, h):
                    copy.wait_recv()

    @pl.when(jnp.logical_not(first))
    def _():
        lax.fori_loop(0, M, stem_out, 0)

    for k in range(S):
        for h in range(T):

            @pl.when((col != k) | (strip != h))
            def _():
                for m in range(M):
                    g_copy(k, h, m, k, h).wait_recv()

    for h in range(T):
        total = gs_recv[0, h]
        for k in range(1, S):
            total = total + gs_recv[k, h]
        o_stem[h * M : (h + 1) * M] = total

    sum_a = sum_d = sum_k = 0.0
    for q in range(Q):
        for h in range(T):
            sum_a = sum_a + far_a[q, h]
            sum_d = sum_d + far_d[q, h]
            sum_k = sum_k + far_k[q, h]
    o_up[...] = sum_a[0 : C2 // n]
    o_mix[...] = sum_a[p2 : p2 + C1 // n]
    o_down[...] = sum_d[0 : C1 // n]
    w = C1 // n
    share = sum_k[0:9, 0:w]
    for k in range(1, n):
        share = jnp.where(dp * T + strip == k, sum_k[0:9, k * w : (k + 1) * w], share)
    o_taps[...] = share

    for m in range(M):
        for h in range(T):

            @pl.when(strip != h)
            def _():
                stem_copy(h, m, strip).wait_send()
                lab_copy(h, m, strip).wait_send()

                @pl.when(jnp.logical_not(last))
                def _():
                    lab_copy(h, m, h).wait_recv()

        @pl.when(jnp.logical_not(last))
        def _():
            f_copy(1, m).wait_send()
            f_copy(2, m).wait_send()
            for r in range(rows):
                f_row(m, r).wait_send()

        @pl.when(jnp.logical_not(first))
        def _():
            b_copy(1, m).wait_send()
            b_copy(2, m).wait_send()
            for r in range(rows):
                b_row(m, r).wait_send()

    for k in range(S):
        for h in range(T):

            @pl.when((col != k) | (strip != h))
            def _():
                for m in range(M):
                    g_copy(k, h, m, col, strip).wait_send()

    for q in range(Q):
        for copy in a_copies(q):
            copy.wait_send()
        for h in range(T):

            @pl.when((mine != q) | (strip != h))
            def _():
                for copy in r_copies(q, h, mine, strip):
                    copy.wait_send()


def finish(*refs):
    for source, target in zip(refs[:4], refs[5:9]):
        target[...] = source[...].reshape(target.shape)
    refs[9][...] = refs[4][...]


def shards(stem, labels, up, mix, down, taps, gain1, gain2, lat1, lat2, cls):
    B, rl, W, C1 = stem.shape
    C2 = up.shape[1]
    S, D, T = lax.axis_size("col"), lax.axis_size("dp"), lax.axis_size("strip")
    M = B // T
    RW = rl * W
    pix = T * RW
    small = pix // 4
    wc = W // S
    n = D * T
    Q = D // 2
    p1, p2 = up_to(C1 // n, 16), up_to(C2 // n, 16)
    npix = float(B * D * rl * T * W)
    V = pltpu.VMEM
    dma = pltpu.SemaphoreType.DMA
    vspec = pl.BlockSpec(memory_space=pltpu.VMEM)
    outs = pl.pallas_call(
        functools.partial(kernel, S, D, T, M, rl, W, npix),
        out_shape=(
            jax.ShapeDtypeStruct((C2 // n, C1), f32),
            jax.ShapeDtypeStruct((C1 // n, C1), f32),
            jax.ShapeDtypeStruct((C1 // n, C2), f32),
            jax.ShapeDtypeStruct((9, C1 // n), f32),
            jax.ShapeDtypeStruct((B, rl, wc, C1), f32),
        ),
        in_specs=[vspec] * 11,
        out_specs=(vspec,) * 5,
        scratch_shapes=[
            V((T, M, RW, C1), f32),
            V((M, T, RW, C1), f32),
            V((M, T, rl, W), jnp.int32),
            V((M, pix, C1), f32),
            V((M, small, C2), f32),
            V((M, pix, C1), f32),
            V((M, small, C2), f32),
            V((M, pix, C1), f32),
            V((M, small, C2), f32),
            V((M, pix, C1), f32),
            V((M, small, C2), f32),
            V((M, small, C1), f32),
            V((M, small, C1), f32),
            V((M, small, C1), f32),
            V((M, small, C1), f32),
            V((M, pix, C1), f32),
            V((M * pix, n * p1), bf16),
            V((M * small, n * p1), bf16),
            V((M * small, n * p2), bf16),
            V((pix + 16, C1), f32),
            V((M, pix, C1), f32),
            V((M, pix, C1), f32),
            V((M, pix, C1), bf16),
            V((M, small, C2), bf16),
            V((M, small, C1), bf16),
            V((M, small, C2), f32),
            V((M, pix, C1), bf16),
            V((M, small, C2), bf16),
            V((M, small, C1), bf16),
            V((pix, small), bf16),
            V((small, pix), bf16),
            V((S, T, M, rl, wc, C1), f32),
            V((S, T, M, rl, wc, C1), f32),
            V((Q, 2, T, p1 + p2, C1), f32),
            V((Q, 2, T, p1, C2), f32),
            V((16, C1), f32),
            V((Q, T, p1 + p2, C1), f32),
            V((Q, T, p1, C2), f32),
            V((16, C1), f32),
            V((Q, T, p1 + p2, C1), f32),
            V((Q, T, p1, C2), f32),
            V((Q, T, 16, C1), f32),
            dma((T, M)),
            dma((T, M)),
            dma((T, M)),
            dma((T, M)),
            dma((3, M)),
            dma((3, M)),
            dma((3, M)),
            dma((3, M)),
            dma((S, T, M)),
            dma((S, T, M)),
            dma((Q + 1, 2)),
            dma((Q + 1, 2)),
            dma((Q, T, 3)),
            dma((Q, T, 3)),
            dma((M, T * rl)),
            dma((M, T * rl)),
            dma((M, T * rl)),
            dma((M, T * rl)),
        ],
        compiler_params=pltpu.CompilerParams(
            collective_id=0, has_side_effects=True, vmem_limit_bytes=60000 * 1024
        ),
        name="columns",
    )(
        stem.reshape(B, RW, C1), labels, up[0], mix[0], down[0], taps[0], gain1, gain2,
        lat1, lat2, cls.T,
    )
    tall = lambda a: jax.ShapeDtypeStruct((a.shape[0], 1, a.shape[1]), f32)
    done = pl.pallas_call(
        finish,
        out_shape=tuple(tall(a) for a in outs[:4])
        + (jax.ShapeDtypeStruct(outs[4].shape, f32),),
        in_specs=[vspec] * 5,
        out_specs=(vspec,) * 5,
        name="finish",
    )(*outs)
    return tuple(jnp.transpose(a, (1, 0, 2)) for a in done[:4]) + (done[4],)


def solution(mesh):
    placed = (
        P("dp", "strip", None, None),
        P("dp", "strip", None),
        P("col", None, None),
        P("col", None, None),
        P("col", None, None),
        P("col", None, None),
        P("col", None),
        P("col", None),
        P(),
        P(),
        P(),
    )
    return jax.shard_map(
        shards,
        mesh=mesh,
        in_specs=placed,
        out_specs=(
            P("col", ("dp", "strip"), None),
            P("col", ("dp", "strip"), None),
            P("col", ("dp", "strip"), None),
            P("col", None, ("dp", "strip")),
            P("dp", "strip", "col", None),
        ),
        check_vma=False,
    )
```
